32 devices in a mesh: row: 4 (over y, x), col: 8 (over z, core).
Axes of the slice: x: 2, y: 2, z: 4, core: 2. Of those that a mesh axis runs over, the one named last changes fastest.
Arguments:
- block_tiles: bfloat16 [4, 160, 128, 128], P('row', 'col'), may hold values from -0.31622777 to 0.31622777
- block_rows: int32 [4, 160], P('row', 'col'), may hold values from 0 to 15, as said below
- block_cols: int32 [4, 160], P('row', 'col'), may hold values from 0 to 7, as said below
- counts: int32 [4, 8], P('row', 'col'), may hold values from 1 to 20, as said below
- start_basis: bfloat16 [8192, 256], P('col'), may hold values from -6 to 6
Outputs:
- image_out: bfloat16 [8192, 256], P(('row', 'col'))
- basis_out: bfloat16 [8192, 256], P(('col', 'row'))
The draws below stay inside these ranges and needn't reach their ends.
Inputs may be any that keep to these rules, and one draw needn't show every extreme that they name: `block_rows`: each entry lies in 0 to 15; within the 20 slots of one slab pair no pair of block row and block column repeats. `block_cols`: each entry lies in 0 to 7; see block_rows. `counts`: some slab pair has all 20 slots live in every draw.
All inputs are finite; a program needn't handle non-finite values.
Results may differ from the reference program's by a relative error of at most 0.025.
Values may be sent and summed in bfloat16 or wider, within the bound.
No kernel may reach another device: no remote copies, remote signals or barrier semaphores. Data moves between devices by JAX's collectives and lax.ppermute only.
A program may use at most 64 MiB of HBM per device.

```python
import jax
import jax.numpy as jnp
from jax import lax

BLOCK = 128
RANK = 256
BRD = 16
BCD = 8
NB = 20
MROWS = 8192
NCOLS = 8192
N_ROW = 4
N_COL = 8


def pair_slots(key):
    subkeys = jax.random.split(jax.random.fold_in(key, 11), N_ROW * N_COL)
    orders = jax.vmap(lambda sub: jax.random.permutation(sub, BRD * BCD)[:NB])(subkeys)
    return orders.reshape(N_ROW, N_COL * NB).astype(jnp.int32)


def draw_block_rows(key, part):
    return (pair_slots(key) // BCD).astype(jnp.int32)


def draw_block_cols(key, part):
    return (pair_slots(key) % BCD).astype(jnp.int32)


def draw_counts(key, part):
    quarters = jax.random.randint(jax.random.fold_in(key, 3), (N_ROW * N_COL,), 1, 5)
    loads = jnp.maximum(NB * quarters // 4, 1)
    chosen = jax.random.randint(jax.random.fold_in(key, 5), (), 0, N_ROW * N_COL)
    loads = jnp.where(jnp.arange(N_ROW * N_COL) == chosen, NB, loads)
    return loads.reshape(N_ROW, N_COL).astype(jnp.int32)


def draw_block_tiles(key, part):
    base = (BLOCK * NB * N_COL // (2 * BRD)) ** (-0.5)
    shape = (N_ROW, N_COL * NB, BLOCK, BLOCK)
    slab = (jnp.arange(N_COL * NB) // NB).astype(jnp.float32)
    position = slab / max(N_COL - 1, 1) - 0.5
    ratio = 2.5
    values = jax.random.normal(jax.random.fold_in(key, 21), shape, jnp.float32)
    values = jnp.clip(values, -4.0, 4.0)
    scales = jnp.exp(jnp.log(ratio) * position)
    scales = scales / jnp.sqrt(jnp.mean(scales * scales))
    return (values * base * scales[None, :, None, None]).astype(jnp.bfloat16)


def block_scale(own_key, shape, cuts, smallest, largest):
    def one(axis_at, shards_of):
        steps = jax.random.uniform(jax.random.fold_in(jax.random.fold_in(own_key, 6), axis_at), (shards_of,), jnp.float32, smallest / len(cuts), largest / len(cuts))
        return jnp.repeat(jnp.exp(steps), shape[axis_at] // shards_of).reshape((-1,) + (1,) * (len(shape) - axis_at - 1))

    factor_of = one(*cuts[0])
    for cut in cuts[1:]:
        factor_of = factor_of * one(*cut)
    return factor_of


def centred(stream_key, shape, deviation, reach, cuts=(), kind=jnp.bfloat16):
    entries = jax.random.normal(stream_key, shape, jnp.float32) * deviation
    if len(cuts) > 0:
        entries = block_scale(stream_key, shape, cuts, -0.22, 0.18) * entries
    return jnp.clip(entries, min=-reach, max=reach).astype(kind)


def setup_inputs(seed: int = 0) -> dict:
    streams_of = jax.random.split(jax.random.key(seed), 6)
    return {
        "block_tiles": draw_block_tiles(jax.random.fold_in(streams_of[5], 71), 0),
        "block_rows": draw_block_rows(jax.random.fold_in(streams_of[5], 71), 0),
        "block_cols": draw_block_cols(jax.random.fold_in(streams_of[5], 71), 0),
        "counts": draw_counts(jax.random.fold_in(streams_of[5], 71), 0),
        "start_basis": centred(streams_of[4], (NCOLS, RANK), 1.0, 6.0, ((0, 8),)),
    }


def one_hot(indices, width):
    return (indices[..., None] == jnp.arange(width, dtype=jnp.int32)).astype(jnp.float32)

def round_half(value):
    return lax.optimization_barrier(value.astype(jnp.bfloat16)).astype(jnp.float32)

def forward(tiles_all, rows_all, cols_all, live_all, basis_slab):
    basis_parts = basis_slab.reshape(N_COL, BCD, BLOCK, RANK)
    column_ids = jnp.arange(N_COL, dtype=jnp.int32)[:, None]

    def per_row(packed):
        row_tiles, row_ids, col_ids, live_slots = packed
        gathered = basis_parts[column_ids, col_ids].astype(jnp.float32)
        products = jnp.einsum('cnij,cnjk->cnik', row_tiles.astype(jnp.float32), gathered)
        select = one_hot(row_ids, BRD) * live_slots[..., None]
        partial_value = jnp.einsum('cna,cnik->caik', select, products, precision=lax.Precision.HIGHEST)
        summed = lax.optimization_barrier(jnp.sum(round_half(partial_value), axis=0))
        return summed.reshape(BRD * BLOCK, RANK).astype(jnp.bfloat16)
    return lax.map(per_row, (tiles_all, rows_all, cols_all, live_all)).reshape(MROWS, RANK)

def backward(tiles_all, rows_all, cols_all, live_all, image_slab):
    image_parts = image_slab.reshape(N_ROW, BRD, BLOCK, RANK)
    row_numbers = jnp.arange(N_ROW, dtype=jnp.int32)[:, None]

    def per_col(packed):
        col_tiles, row_ids, col_ids, live_slots = packed
        gathered = image_parts[row_numbers, row_ids].astype(jnp.float32)
        products = jnp.einsum('rnij,rnik->rnjk', col_tiles.astype(jnp.float32), gathered)
        select = one_hot(col_ids, BCD) * live_slots[..., None]
        partial_value = jnp.einsum('rnb,rnjk->rbjk', select, products, precision=lax.Precision.HIGHEST)
        summed = lax.optimization_barrier(jnp.sum(round_half(partial_value), axis=0))
        return summed.reshape(BCD * BLOCK, RANK)
    swapped = (jnp.swapaxes(tiles_all, 0, 1), jnp.swapaxes(rows_all, 0, 1), jnp.swapaxes(cols_all, 0, 1), jnp.swapaxes(live_all, 0, 1))
    return lax.map(per_col, swapped).reshape(NCOLS, RANK)

def normalize(summed):
    mean_square = lax.optimization_barrier(jnp.mean(summed * summed, axis=0))
    return (summed / jnp.sqrt(mean_square + 1e-06)).astype(jnp.bfloat16)

def reference(block_tiles, block_rows, block_cols, counts, start_basis):
    tiles_all = block_tiles.reshape(N_ROW, N_COL, NB, BLOCK, BLOCK)
    rows_all = block_rows.reshape(N_ROW, N_COL, NB).astype(jnp.int32)
    cols_all = block_cols.reshape(N_ROW, N_COL, NB).astype(jnp.int32)
    live_all = (jnp.arange(NB, dtype=jnp.int32)[None, None, :] < counts[:, :, None]).astype(jnp.float32)
    image_first = forward(tiles_all, rows_all, cols_all, live_all, start_basis)
    basis_first = normalize(backward(tiles_all, rows_all, cols_all, live_all, image_first))
    image_out = forward(tiles_all, rows_all, cols_all, live_all, basis_first)
    basis_out = normalize(backward(tiles_all, rows_all, cols_all, live_all, image_out))
    return (image_out, basis_out)
```

```python
import functools

import jax
import jax.numpy as jnp
from jax import lax
from jax.experimental import pallas as pl
from jax.experimental.pallas import tpu as pltpu
from jax.sharding import PartitionSpec as P

BF = jnp.bfloat16
F32 = jnp.float32


def block_product(ids, tiles, parts, out_blocks, transposed, scale_parts=(), total=None, want_sum=False,
                  want_value=False):
    groups = len(tiles)
    slots, size, _ = tiles[0].shape
    in_blocks, width, _ = parts[0].shape
    n_parts = len(parts)
    n_scale = len(scale_parts)
    contract = (((1,), (0,)), ((), ())) if transposed else (((1,), (1,)), ((), ()))

    def body(*refs):
        ids_ref = refs[0]
        tile_refs = refs[1:1 + groups]
        part_refs = refs[1 + groups:1 + groups + n_parts]
        scale_refs = refs[1 + groups + n_parts:1 + groups + n_parts + n_scale]
        rest = list(refs[1 + groups + n_parts + n_scale:])
        out_ref = rest.pop(0)
        sum_ref = rest.pop(0) if want_sum else None
        value_ref = rest.pop(0) if want_value else None
        tile_buf, operand, acc, sems = rest
        for g in range(groups):
            pltpu.make_async_copy(tile_refs[g], tile_buf.at[g], sems.at[g]).start()
        acc[...] = jnp.zeros_like(acc)
        if n_scale:
            squares = scale_refs[0][...]
            for ref in scale_refs[1:]:
                squares = squares + ref[...]
            scale = lax.rsqrt(jnp.sum(squares, axis=1, keepdims=True) / total + 1e-6)

        def gather_operand(i, carry):
            value = part_refs[0][i].astype(F32)
            for ref in part_refs[1:]:
                value = value + ref[i].astype(F32)
            if n_scale:
                value = value * scale
            operand[i] = value.astype(BF)
            if want_value:
                value_ref[i] = value.astype(BF)
            return carry + value * value if want_sum else carry

        squares_out = lax.fori_loop(
            0, in_blocks, gather_operand, jnp.zeros((width, size), F32) if want_sum else 0, unroll=4)
        if want_sum:
            sum_ref[...] = squares_out

        def group(g, carry):
            pltpu.make_async_copy(tile_buf.at[g], tile_buf.at[g], sems.at[g]).wait()
            for s in range(slots):
                to = ids_ref[g, 0, s]
                source = ids_ref[g, 1, s]
                acc[to] += lax.dot_general(
                    operand[source], tile_buf[g, s], contract, preferred_element_type=F32)
            return carry

        lax.fori_loop(0, groups, group, 0)
        out_ref[...] = acc[0:out_blocks].astype(BF)

    out_shape = [jax.ShapeDtypeStruct((out_blocks, width, size), BF)]
    if want_sum:
        out_shape.append(jax.ShapeDtypeStruct((width, size), F32))
    if want_value:
        out_shape.append(jax.ShapeDtypeStruct((in_blocks, width, size), BF))
    vmem = pl.BlockSpec(memory_space=pltpu.VMEM)
    return pl.pallas_call(
        body,
        out_shape=out_shape,
        in_specs=[pl.BlockSpec(memory_space=pltpu.SMEM)]
        + [pl.BlockSpec(memory_space=pl.ANY)] * groups
        + [vmem] * (n_parts + n_scale),
        out_specs=[vmem] * len(out_shape),
        scratch_shapes=[
            pltpu.VMEM((groups, slots, size, size), BF),
            pltpu.VMEM((in_blocks, width, size), BF),
            pltpu.VMEM((out_blocks + 1, width, size), F32),
            pltpu.SemaphoreType.DMA((groups,)),
        ],
        name="backward" if transposed else "forward",
    )(ids, *tiles, *parts, *scale_parts)


def shards(n_row, n_col, slab_rows, block_tiles, block_rows, block_cols, counts, start_basis):
    tiles = block_tiles[0]
    slots, size, _ = tiles.shape
    slab_cols, rank = start_basis.shape
    row_blocks = slab_rows // size
    col_blocks = slab_cols // size
    n_z = n_col // 2
    width = rank // 8
    out_rows = 2 * row_blocks
    out_cols = 4 * col_blocks
    row = lax.axis_index("row")
    col = lax.axis_index("col")
    x = row % 2
    z = (col // 2) % 2
    core = col % 2
    half_z = col // 4
    half_row = row // 2

    def flip(dx, dz, dc):
        return [(r * n_col + c, (r ^ dx) * n_col + (c ^ (2 * dz + dc)))
                for r in range(n_row) for c in range(n_col)]

    def send(value, dx, dz, dc):
        return lax.ppermute(value, ("row", "col"), flip(dx, dz, dc))

    def others_z(value):
        return [
            lax.ppermute(value, "col", [(c, (c + 4 * k) % n_col) for c in range(n_col)])
            for k in range(1, n_col // 4)
        ]

    def others_row(value):
        return [
            lax.ppermute(value, "row", [(r, (r + 2 * k) % n_row) for r in range(n_row)])
            for k in range(1, n_row // 2)
        ]

    own = [tiles, send(tiles, 1, 0, 0), send(tiles, 0, 1, 0), send(tiles, 1, 1, 0)]
    twin = [send(t, 0, 0, 1) for t in own]

    live = jnp.arange(slots, dtype=jnp.int32)[None] < counts[0, 0]
    row_ids = x * row_blocks + block_rows
    col_ids = (2 * z + core) * col_blocks + block_cols
    ids = jnp.stack([
        jnp.where(live, row_ids, out_rows), col_ids, jnp.where(live, col_ids, out_cols), row_ids], axis=1)
    ids = jnp.concatenate([ids, send(ids, 0, 0, 1)])
    ids = jnp.concatenate([ids, send(ids, 0, 1, 0)])
    ids = jnp.concatenate([ids, send(ids, 1, 0, 0)])
    forward_ids, backward_ids = ids[:, 0:2], ids[:, 2:4]
    all_tiles = [t for pair in zip(own, twin) for t in pair]
    all_tiles = all_tiles[0:2] + all_tiles[4:6] + all_tiles[2:4] + all_tiles[6:8]

    start = start_basis.reshape(col_blocks, size, 2, 2, 2, width).transpose(2, 3, 4, 0, 5, 1)
    start = lax.dynamic_index_in_dim(start, x, 0, keepdims=False)
    near = lax.dynamic_index_in_dim(start, core, 1, keepdims=False)
    far = send(lax.dynamic_index_in_dim(start, 1 - core, 1, keepdims=False), 0, 0, 1)
    start = jnp.where(core == 0, jnp.stack([near, far], 1), jnp.stack([far, near], 1))
    near = lax.dynamic_index_in_dim(start, z, 0, keepdims=False)
    far = send(lax.dynamic_index_in_dim(start, 1 - z, 0, keepdims=False), 0, 1, 0)
    basis = jnp.where(z == 0, jnp.stack([near, far]), jnp.stack([far, near]))
    basis = basis.reshape(out_cols, width, size)

    total = n_col * slab_cols
    (image,) = block_product(forward_ids, all_tiles, [basis], out_rows, False)
    (basis,) = block_product(backward_ids, all_tiles, [image] + others_z(image), out_cols, True)
    image, squares = block_product(
        forward_ids, all_tiles, [basis] + others_row(basis), out_rows, False, want_sum=True)
    basis, value = block_product(
        backward_ids, all_tiles, [image] + others_z(image), out_cols, True,
        scale_parts=[squares] + others_z(squares), total=total, want_value=True)
    basis = [basis] + others_row(basis)
    basis = functools.reduce(jnp.add, [b.astype(F32) for b in basis])
    squares = jnp.sum(jnp.sum(basis * basis, axis=0), axis=1, keepdims=True)
    squares = functools.reduce(jnp.add, [squares] + others_z(squares))
    basis = (basis * lax.rsqrt(squares / total + 1e-6)).astype(BF)

    def deliver(value, lead, at, keep_axis):
        rows = value.shape[0] * size // (8 * lead)
        lanes = min(rows, size)
        if rows >= size:
            pieces = value.reshape((value.shape[0] * size // rows, rows // size, width, size))
        else:
            pieces = value.reshape(value.shape[0], width, size // rows, rows).transpose(0, 2, 1, 3)
            pieces = pieces.reshape(-1, 1, width, rows)
        pieces = keep_axis(pieces, at)
        sub = rows // lanes
        pieces = pieces.reshape(2, 2, 2, sub, width, lanes)
        near = lax.dynamic_index_in_dim(pieces, core, 2, keepdims=False)
        far = send(lax.dynamic_index_in_dim(pieces, 1 - core, 2, keepdims=False), 0, 0, 1)
        pieces = jnp.where(core == 0, jnp.stack([near, far], 2), jnp.stack([far, near], 2))

        def pick(dx, dz):
            piece = lax.dynamic_index_in_dim(pieces, x ^ dx, 0, keepdims=False)
            return lax.dynamic_index_in_dim(piece, z ^ dz, 0, keepdims=False)

        got = [[pick(0, 0), send(pick(0, 1), 0, 1, 0)], [send(pick(1, 0), 1, 0, 0), send(pick(1, 1), 1, 1, 0)]]
        got = [jnp.where(z == 0, jnp.stack(g), jnp.stack(g[::-1])) for g in got]
        got = jnp.where(x == 0, jnp.stack(got), jnp.stack(got[::-1]))
        got = got.reshape(8, sub, width, lanes).transpose(1, 3, 0, 2)
        return got.reshape(rows, rank)

    def image_pieces(pieces, at):
        pieces = pieces.reshape((2, n_z // 2, 4) + pieces.shape[1:])
        return lax.dynamic_index_in_dim(pieces, at, 1, keepdims=False)

    def basis_pieces(pieces, at):
        pieces = pieces.reshape((4, n_row // 2, 2) + pieces.shape[1:])
        pieces = lax.dynamic_index_in_dim(pieces, at, 1, keepdims=False)
        return jnp.moveaxis(pieces, 1, 0)

    image_piece = deliver(value, n_z // 2, half_z, image_pieces)
    basis_piece = deliver(basis, n_row // 2, half_row, basis_pieces)
    return image_piece, basis_piece


def solution(mesh):
    n_row, n_col = mesh.shape["row"], mesh.shape["col"]

    def whole(block_tiles, block_rows, block_cols, counts, start_basis):
        slab_rows = start_basis.shape[0] // n_row
        return jax.shard_map(
            functools.partial(shards, n_row, n_col, slab_rows),
            mesh=mesh,
            in_specs=(
                P("row", "col", None, None),
                P("row", "col"),
                P("row", "col"),
                P("row", "col"),
                P("col", None),
            ),
            out_specs=(P(("row", "col"), None), P(("col", "row"), None)),
            check_vma=False,
        )(block_tiles, block_rows, block_cols, counts, start_basis)

    return whole
```

```python
import functools
import math

import jax
import jax.numpy as jnp
from jax import lax
from jax.experimental import pallas as pl
from jax.experimental.pallas import tpu as pltpu
from jax.sharding import PartitionSpec as P

BF = jnp.bfloat16
F32 = jnp.float32


def in_vmem(value):
    return pltpu.with_memory_space_constraint(value, pltpu.VMEM)


def block_product(ids, tiles, parts, out_blocks, transposed, scale_parts=(), total=None, want_sum=False,
                  want_value=False):
    size = tiles[0].shape[1]
    in_blocks, width, _ = parts[0].shape
    n_tiles, n_parts, n_scale = len(tiles), len(parts), len(scale_parts)
    unroll = functools.reduce(math.gcd, [t.shape[0] for t in tiles])
    contract = (((1,), (0,)), ((), ())) if transposed else (((1,), (1,)), ((), ()))

    def body(*refs):
        ids_ref = refs[0]
        tile_refs = refs[1:1 + n_tiles]
        part_refs = refs[1 + n_tiles:1 + n_tiles + n_parts]
        scale_refs = refs[1 + n_tiles + n_parts:1 + n_tiles + n_parts + n_scale]
        rest = list(refs[1 + n_tiles + n_parts + n_scale:])
        out_ref = rest.pop(0)
        sum_ref = rest.pop(0) if want_sum else None
        value_ref = rest.pop(0) if want_value else None
        operand, acc = rest
        acc[...] = jnp.zeros_like(acc)
        if n_scale:
            squares = scale_refs[0][...]
            for ref in scale_refs[1:]:
                squares = squares + ref[...]
            scale = lax.rsqrt(jnp.sum(squares, axis=1, keepdims=True) / total + 1e-6)

        def gather_operand(i, carry):
            value = part_refs[0][i].astype(F32)
            for ref in part_refs[1:]:
                value = value + ref[i].astype(F32)
            if n_scale:
                value = value * scale
            operand[i] = value.astype(BF)
            if want_value:
                value_ref[i] = value.astype(BF)
            return carry + value * value if want_sum else carry

        squares_out = lax.fori_loop(
            0, in_blocks, gather_operand, jnp.zeros((width, size), F32) if want_sum else 0, unroll=4)
        if want_sum:
            sum_ref[...] = squares_out

        at = 0
        for ref in tile_refs:
            def some(i, carry, ref=ref, at=at):
                for s in range(unroll):
                    slot = i * unroll + s
                    to = ids_ref[at + slot, 0]
                    source = ids_ref[at + slot, 1]
                    acc[to] += lax.dot_general(
                        operand[source], ref[slot], contract, preferred_element_type=F32)
                return carry

            lax.fori_loop(0, ref.shape[0] // unroll, some, 0)
            at += ref.shape[0]
        out_ref[...] = acc[0:out_blocks].astype(BF)

    out_shape = [pltpu.VMEM((out_blocks, width, size), BF)]
    if want_sum:
        out_shape.append(pltpu.VMEM((width, size), F32))
    if want_value:
        out_shape.append(pltpu.VMEM((in_blocks, width, size), BF))
    vmem = pl.BlockSpec(memory_space=pltpu.VMEM)
    return pl.pallas_call(
        body,
        out_shape=out_shape,
        in_specs=[pl.BlockSpec(memory_space=pltpu.SMEM)] + [vmem] * (n_tiles + n_parts + n_scale),
        out_specs=[vmem] * len(out_shape),
        scratch_shapes=[
            pltpu.VMEM((in_blocks, width, size), BF),
            pltpu.VMEM((out_blocks + 1, width, size), F32),
        ],
        compiler_params=pltpu.CompilerParams(vmem_limit_bytes=8 * 1024 * 1024),
        name="backward" if transposed else "forward",
    )(ids, *[in_vmem(t) for t in (*tiles, *parts, *scale_parts)])


def shards(n_row, n_col, slab_rows, block_tiles, block_rows, block_cols, counts, start_basis):
    tiles = block_tiles[0]
    slots, size, _ = tiles.shape
    slab_cols, rank = start_basis.shape
    row_blocks = slab_rows // size
    col_blocks = slab_cols // size
    width = rank // 8
    out_rows = 2 * row_blocks
    out_cols = 4 * col_blocks
    row = lax.axis_index("row")
    col = lax.axis_index("col")
    x = row % 2
    z = (col // 2) % 2
    core = col % 2
    half_z = col // 4
    half_row = row // 2

    def send(value, dx, dz, dc):
        return lax.ppermute(value, ("row", "col"), [
            (r * n_col + c, (r ^ dx) * n_col + (c ^ (2 * dz + dc)))
            for r in range(n_row) for c in range(n_col)])

    def others_z(value):
        return [
            lax.ppermute(value, "col", [(c, (c + 4 * k) % n_col) for c in range(n_col)])
            for k in range(1, n_col // 4)
        ]

    def others_row(value):
        return [
            lax.ppermute(value, "row", [(r, (r + 2 * k) % n_row) for r in range(n_row)])
            for k in range(1, n_row // 2)
        ]

    half = slots // 2
    tiles_x = send(tiles, 1, 0, 0)
    tiles_z = send(tiles, 0, 1, 0)
    ids = jnp.stack([
        jnp.where(jnp.arange(slots, dtype=jnp.int32) < counts[0, 0], block_rows[0], -1), block_cols[0]], axis=1)
    ids = jnp.stack([ids, send(ids, 0, 0, 1)])
    ids_x = send(ids, 1, 0, 0)
    ids_z = send(ids, 0, 1, 0)
    ids_xz = send(ids, 1, 1, 0)

    start = start_basis.reshape(col_blocks, size, 8, width).transpose(2, 0, 3, 1)

    def chunk(dz, dc):
        return lax.dynamic_index_in_dim(start, 4 * x + 2 * (z ^ dz) + (core ^ dc), 0, keepdims=False)

    twin_start = send(jnp.stack([chunk(0, 1), chunk(1, 1)]), 0, 0, 1)
    basis_z = send(jnp.stack([chunk(1, 0), twin_start[1]]), 0, 1, 0)
    basis = jnp.concatenate([chunk(0, 0)[None], twin_start[0:1], basis_z]).reshape(out_cols, width, size)

    corner_a = send(tiles_x[:half], 0, 1, 0)
    corner_b = send(tiles_z[half:], 1, 0, 0)
    all_tiles = []
    for t in (tiles, tiles_x, tiles_z, corner_a, corner_b):
        all_tiles += [t, send(t, 0, 0, 1)]

    def index(found, dx, dz, dc):
        live = found[:, 0] >= 0
        to_row = found[:, 0] + dx * row_blocks
        to_col = found[:, 1] + (2 * dz + dc) * col_blocks
        return jnp.stack([
            jnp.where(live, to_row, out_rows), to_col,
            jnp.where(live, to_col, out_cols), jnp.where(live, to_row, 0)], axis=1)

    indices = []
    for found, dx, dz in ((ids, 0, 0), (ids_x, 1, 0), (ids_z, 0, 1), (ids_xz[:, :half], 1, 1), (ids_xz[:, half:], 1, 1)):
        indices += [index(found[0], dx, dz, 0), index(found[1], dx, dz, 1)]
    indices = jnp.concatenate(indices)
    forward_ids, backward_ids = indices[:, 0:2], indices[:, 2:4]

    total = n_col * slab_cols
    (image,) = block_product(forward_ids, all_tiles, [basis], out_rows, False)
    (basis,) = block_product(backward_ids, all_tiles, [image] + others_z(image), out_cols, True)
    image, squares = block_product(
        forward_ids, all_tiles, [basis] + others_row(basis), out_rows, False, want_sum=True)
    basis, value = block_product(
        backward_ids, all_tiles, [image] + others_z(image), out_cols, True,
        scale_parts=[squares] + others_z(squares), total=total, want_value=True)
    basis = [basis] + others_row(basis)
    basis = functools.reduce(jnp.add, [b.astype(F32) for b in basis])
    squares = jnp.sum(jnp.sum(basis * basis, axis=0), axis=1, keepdims=True)
    squares = functools.reduce(jnp.add, [squares] + others_z(squares))
    basis = (basis * lax.rsqrt(squares / total + 1e-6)).astype(BF)

    image_rows = slab_rows // n_col
    basis_rows = slab_cols // n_row
    image_span = max(image_rows // size, 1)
    basis_span = max(basis_rows // size, 1)
    value = value.reshape(2, row_blocks, width, size)
    basis = basis.reshape(2, 2, col_blocks, width, size)

    def pieces(dc):
        out = []
        for dx in range(2):
            for dz in range(2):
                first = (4 * half_z + 2 * (z ^ dz) + (core ^ dc)) * image_rows // size
                out.append(lax.dynamic_slice_in_dim(value[dx], first, image_span, 0))
                first = (2 * half_row + (x ^ dx)) * basis_rows // size
                out.append(lax.dynamic_slice_in_dim(basis[dz, dc], first, basis_span, 0))
        return jnp.concatenate(out).reshape(2, 2, image_span + basis_span, width, size)

    keep = pieces(0)
    twin = send(pieces(1), 0, 0, 1)
    got = [[jnp.stack([keep[dx, dz], twin[dx, dz]]) for dz in range(2)] for dx in range(2)]
    got = [[got[0][0], send(got[0][1], 0, 1, 0)], [send(got[1][0], 1, 0, 0), send(got[1][1], 1, 1, 0)]]
    got = [[jnp.where(core == 0, g, g[::-1]) for g in row_of] for row_of in got]
    got = [jnp.where(z == 0, jnp.stack(g), jnp.stack(g[::-1])) for g in got]
    got = jnp.where(x == 0, jnp.stack(got), jnp.stack(got[::-1]))
    got = got.reshape(8, image_span + basis_span, width, size).transpose(1, 3, 0, 2)
    got = got.reshape((image_span + basis_span) * size, rank)
    image_piece = got[:image_span * size]
    basis_piece = got[image_span * size:]
    if image_rows < size:
        image_piece = lax.dynamic_slice_in_dim(image_piece, col * image_rows % size, image_rows, 0)
    if basis_rows < size:
        basis_piece = lax.dynamic_slice_in_dim(basis_piece, row * basis_rows % size, basis_rows, 0)
    return image_piece, basis_piece


def solution(mesh):
    n_row, n_col = mesh.shape["row"], mesh.shape["col"]

    def whole(block_tiles, block_rows, block_cols, counts, start_basis):
        slab_rows = start_basis.shape[0] // n_row
        return jax.shard_map(
            functools.partial(shards, n_row, n_col, slab_rows),
            mesh=mesh,
            in_specs=(
                P("row", "col", None, None),
                P("row", "col"),
                P("row", "col"),
                P("row", "col"),
                P("col", None),
            ),
            out_specs=(P(("row", "col"), None), P(("col", "row"), None)),
            check_vma=False,
        )(block_tiles, block_rows, block_cols, counts, start_basis)

    return whole
```

```python
import functools
import math

import jax
import jax.numpy as jnp
from jax import lax
from jax.experimental import pallas as pl
from jax.experimental.pallas import tpu as pltpu
from jax.sharding import PartitionSpec as P


BF = jnp.bfloat16
F32 = jnp.float32


def in_vmem(value):
    return pltpu.with_memory_space_constraint(value, pltpu.VMEM)


def first_product(place, found, start, tiles, row_blocks):
    slots, size, _ = tiles.shape
    col_blocks, rank = start.shape[0] // size, start.shape[1]
    width = rank // 8

    def body(place_ref, found_ref, start_ref, tile_ref, keep_ref, send_ref, flipped, acc):
        for c in range(col_blocks):
            flipped[c] = start_ref[c * size:(c + 1) * size, :].T
        acc[...] = jnp.zeros_like(acc)
        for s in range(slots):
            to = found_ref[0, s]
            to = jnp.where(to < 0, row_blocks, to)
            acc[to] += lax.dot_general(
                flipped[found_ref[1, s]], tile_ref[s], (((1,), (1,)), ((), ())), preferred_element_type=F32)
        x, z, core = place_ref[0], place_ref[1], place_ref[2]
        for dx in range(2):
            for dz in range(2):
                at = 4 * jnp.bitwise_xor(x, dx) + 2 * jnp.bitwise_xor(z, dz)
                for ref, mine in ((keep_ref, core), (send_ref, 1 - core)):
                    first = pl.multiple_of((at + mine) * width, width)
                    ref[2 * dx + dz] = acc[0:row_blocks, pl.ds(first, width), :].astype(BF)

    smem = pl.BlockSpec(memory_space=pltpu.SMEM)
    vmem = pl.BlockSpec(memory_space=pltpu.VMEM)
    return pl.pallas_call(
        body,
        out_shape=[pltpu.VMEM((4, row_blocks, width, size), BF)] * 2,
        in_specs=[smem, smem, vmem, vmem],
        out_specs=[vmem, vmem],
        scratch_shapes=[
            pltpu.VMEM((col_blocks, rank, size), BF),
            pltpu.VMEM((row_blocks + 1, rank, size), F32),
        ],
        compiler_params=pltpu.CompilerParams(vmem_limit_bytes=12 * 1024 * 1024),
        name="first",
    )(place, found, in_vmem(start), in_vmem(tiles))


def flip_blocks(tiles):
    count = len(tiles)
    unroll = functools.reduce(math.gcd, [t.shape[0] for t in tiles])

    def body(*refs):
        for ref, out, same in zip(refs[:count], refs[count:2 * count], refs[2 * count:]):
            def some(i, carry, ref=ref, out=out, same=same):
                for s in range(unroll):
                    block = ref[i * unroll + s]
                    out[i * unroll + s] = block.T
                    same[i * unroll + s] = block
                return carry

            lax.fori_loop(0, ref.shape[0] // unroll, some, 0)

    vmem = pl.BlockSpec(memory_space=pltpu.VMEM)
    return pl.pallas_call(
        body,
        out_shape=[pltpu.VMEM(t.shape, t.dtype) for t in (*tiles, *tiles)],
        in_specs=[vmem] * count,
        out_specs=[vmem] * (2 * count),
        compiler_params=pltpu.CompilerParams(vmem_limit_bytes=8 * 1024 * 1024),
        name="flip",
    )(*[in_vmem(t) for t in tiles])


def block_product(ids, which, tiles, parts, out_blocks, scale_parts=(), total=None, want_sum=False, want_value=False):
    size = tiles[0].shape[1]
    in_blocks, width, _ = parts[0].shape
    n_tiles, n_parts, n_scale = len(tiles), len(parts), len(scale_parts)
    contract = (((1,), (0,)), ((), ()))
    runs = [[]]
    for t in range(n_tiles):
        if sum(tiles[u].shape[0] for u in runs[-1]) >= 40:
            runs.append([])
        runs[-1].append(t)

    def body(*refs):
        ids_ref = refs[0]
        tile_refs = refs[1:1 + n_tiles]
        part_refs = refs[1 + n_tiles:1 + n_tiles + n_parts]
        scale_refs = refs[1 + n_tiles + n_parts:1 + n_tiles + n_parts + n_scale]
        rest = list(refs[1 + n_tiles + n_parts + n_scale:])
        out_ref = rest.pop(0)
        sum_ref = rest.pop(0) if want_sum else None
        value_ref = rest.pop(0) if want_value else None
        operand, acc, where, sem = rest
        copy = pltpu.make_async_copy(ids_ref, where, sem)
        copy.start()
        acc[...] = jnp.zeros_like(acc)
        if n_scale:
            squares = scale_refs[0][...]
            for ref in scale_refs[1:]:
                squares = squares + ref[...]
            scale = lax.rsqrt(jnp.sum(squares, axis=1, keepdims=True) / total + 1e-6)

        def gather_operand(i, carry):
            value = part_refs[0][i].astype(F32)
            for ref in part_refs[1:]:
                value = value + ref[i].astype(F32)
            if n_scale:
                value = value * scale
            operand[i] = value.astype(BF)
            if want_value:
                value_ref[i] = value.astype(BF)
            return carry + value * value if want_sum else carry

        squares_out = lax.fori_loop(
            0, in_blocks, gather_operand, jnp.zeros((width, size), F32) if want_sum else 0, unroll=4)
        if want_sum:
            sum_ref[...] = squares_out
        copy.wait()
        slot = 0
        for ref in tile_refs:
            for s in range(ref.shape[0]):
                to = where[which, slot]
                source = where[which + 1, slot]
                acc[to] += lax.dot_general(operand[source], ref[s], contract, preferred_element_type=F32)
                slot += 1
        out_ref[...] = acc[0:out_blocks].astype(BF)

    out_shape = [pltpu.VMEM((out_blocks, width, size), BF)]
    if want_sum:
        out_shape.append(pltpu.VMEM((width, size), F32))
    if want_value:
        out_shape.append(pltpu.VMEM((in_blocks, width, size), BF))
    vmem = pl.BlockSpec(memory_space=pltpu.VMEM)
    return pl.pallas_call(
        body,
        out_shape=out_shape,
        in_specs=[pl.BlockSpec(memory_space=pl.ANY)] + [vmem] * (n_tiles + n_parts + n_scale),
        out_specs=[vmem] * len(out_shape),
        scratch_shapes=[
            pltpu.VMEM((in_blocks, width, size), BF),
            pltpu.VMEM((out_blocks + 1, width, size), F32),
            pltpu.SMEM(ids.shape, jnp.int32),
            pltpu.SemaphoreType.DMA,
        ],
        compiler_params=pltpu.CompilerParams(vmem_limit_bytes=8 * 1024 * 1024),
        name="product",
    )(ids, *[in_vmem(t) for t in (*tiles, *parts, *scale_parts)])


def shards(n_row, n_col, slab_rows, block_tiles, block_rows, block_cols, counts, start_basis):
    tiles = block_tiles[0]
    slots, size, _ = tiles.shape
    slab_cols, rank = start_basis.shape
    row_blocks = slab_rows // size
    col_blocks = slab_cols // size
    width = rank // 8
    out_rows = 2 * row_blocks
    out_cols = 4 * col_blocks
    row = lax.axis_index("row")
    col = lax.axis_index("col")
    x = row % 2
    z = (col // 2) % 2
    core = col % 2
    half_z = col // 4
    half_row = row // 2

    def send(value, dx, dz, dc):
        return lax.ppermute(value, ("row", "col"), [
            (r * n_col + c, (r ^ dx) * n_col + (c ^ (2 * dz + dc)))
            for r in range(n_row) for c in range(n_col)])

    def others_z(value):
        return [
            lax.ppermute(value, "col", [(c, (c + 4 * k) % n_col) for c in range(n_col)])
            for k in range(1, n_col // 4)
        ]

    def others_row(value):
        return [
            lax.ppermute(value, "row", [(r, (r + 2 * k) % n_row) for r in range(n_row)])
            for k in range(1, n_row // 2)
        ]

    tiles_x = send(tiles, 1, 0, 0)
    found = jnp.stack([
        jnp.where(jnp.arange(slots, dtype=jnp.int32) < counts[0, 0], block_rows[0], -1), block_cols[0]])
    keep, other = first_product(jnp.stack([x, z, core]), found, start_basis, tiles, row_blocks)
    image = keep.astype(F32) + send(other, 0, 0, 1).astype(F32)
    image = image.astype(BF).reshape(2, 2, row_blocks, width, size)
    other = image[:, 1]
    image = (image[:, 0].astype(F32) + send(other, 0, 1, 0).astype(F32)).astype(BF)

    tiles_z = send(lax.optimization_barrier((tiles, other))[0], 0, 1, 0)
    image = jnp.concatenate([image[0], send(image[1], 1, 0, 0)])
    image = [image] + others_z(image)
    part = slots // 2
    corner_b = send(tiles_z[part:], 1, 0, 0)
    corner_a = send(lax.optimization_barrier((tiles_x[:part], image[0]))[0], 0, 1, 0)
    all_tiles = []
    for t in (tiles, tiles_x, tiles_z, corner_a, corner_b):
        all_tiles += [t, send(t, 0, 0, 1)]

    found = jnp.stack([found, send(found, 0, 0, 1)])
    found_x = send(found, 1, 0, 0)
    found_z = send(found, 0, 1, 0)
    found_xz = send(found, 1, 1, 0)

    found_x, found_z, found_xz, _ = lax.optimization_barrier((found_x, found_z, found_xz, image[0]))

    def index(at, dx, dz, dc):
        live = at[0] >= 0
        to_row = at[0] + dx * row_blocks
        to_col = at[1] + (2 * dz + dc) * col_blocks
        return jnp.stack([
            jnp.where(live, to_row, out_rows), to_col, jnp.where(live, to_col, out_cols), jnp.where(live, to_row, 0)])

    ids = []
    for at, dx, dz in ((found, 0, 0), (found_x, 1, 0), (found_z, 0, 1), (found_xz[:, :, :part], 1, 1),
                       (found_xz[:, :, part:], 1, 1)):
        ids += [index(at[0], dx, dz, 0), index(at[1], dx, dz, 1)]
    ids = jnp.concatenate(ids, axis=1)

    total = n_col * slab_cols
    (basis,) = block_product(ids, 2, all_tiles, image, out_cols)
    basis = [basis] + others_row(basis)
    flipped = flip_blocks(all_tiles)
    flipped, all_tiles = flipped[:len(all_tiles)], flipped[len(all_tiles):]
    image, squares = block_product(ids, 0, flipped, basis, out_rows, want_sum=True)
    basis, value = block_product(
        ids, 2, all_tiles, [image] + others_z(image), out_cols,
        scale_parts=[squares] + others_z(squares), total=total, want_value=True)
    basis = [basis] + others_row(basis)
    basis = functools.reduce(jnp.add, [b.astype(F32) for b in basis])
    squares = jnp.sum(jnp.sum(basis * basis, axis=0), axis=1, keepdims=True)
    squares = functools.reduce(jnp.add, [squares] + others_z(squares))
    basis = (basis * lax.rsqrt(squares / total + 1e-6)).astype(BF)

    image_rows = slab_rows // n_col
    basis_rows = slab_cols // n_row
    image_span = max(image_rows // size, 1)
    basis_span = max(basis_rows // size, 1)
    value = value.reshape(2, row_blocks, width, size)
    basis = basis.reshape(2, 2, col_blocks, width, size)

    def pieces(dc):
        out = []
        for dx in range(2):
            for dz in range(2):
                first = (4 * half_z + 2 * (z ^ dz) + (core ^ dc)) * image_rows // size
                out.append(lax.dynamic_slice_in_dim(value[dx], first, image_span, 0))
                first = (2 * half_row + (x ^ dx)) * basis_rows // size
                out.append(lax.dynamic_slice_in_dim(basis[dz, dc], first, basis_span, 0))
        return jnp.concatenate(out).reshape(2, 2, image_span + basis_span, width, size)

    keep = pieces(0)
    twin = send(pieces(1), 0, 0, 1)
    got = [[jnp.stack([keep[dx, dz], twin[dx, dz]]) for dz in range(2)] for dx in range(2)]
    got = [[got[0][0], send(got[0][1], 0, 1, 0)], [send(got[1][0], 1, 0, 0), send(got[1][1], 1, 1, 0)]]
    got = [[jnp.where(core == 0, g, g[::-1]) for g in row_of] for row_of in got]
    got = [jnp.where(z == 0, jnp.stack(g), jnp.stack(g[::-1])) for g in got]
    got = jnp.where(x == 0, jnp.stack(got), jnp.stack(got[::-1]))
    got = got.reshape(8, image_span + basis_span, width, size).transpose(1, 3, 0, 2)
    got = got.reshape((image_span + basis_span) * size, rank)
    image_piece = got[:image_span * size]
    basis_piece = got[image_span * size:]
    if image_rows < size:
        image_piece = lax.dynamic_slice_in_dim(image_piece, col * image_rows % size, image_rows, 0)
    if basis_rows < size:
        basis_piece = lax.dynamic_slice_in_dim(basis_piece, row * basis_rows % size, basis_rows, 0)
    return image_piece, basis_piece


def solution(mesh):
    n_row, n_col = mesh.shape["row"], mesh.shape["col"]

    def whole(block_tiles, block_rows, block_cols, counts, start_basis):
        slab_rows = start_basis.shape[0] // n_row
        return jax.shard_map(
            functools.partial(shards, n_row, n_col, slab_rows),
            mesh=mesh,
            in_specs=(
                P("row", "col", None, None),
                P("row", "col"),
                P("row", "col"),
                P("row", "col"),
                P("col", None),
            ),
            out_specs=(P(("row", "col"), None), P(("col", "row"), None)),
            check_vma=False,
        )(block_tiles, block_rows, block_cols, counts, start_basis)

    return whole
```

```python
import functools

import jax
import jax.numpy as jnp
from jax import lax
from jax.experimental import pallas as pl
from jax.experimental.pallas import tpu as pltpu
from jax.sharding import PartitionSpec as P


BF = jnp.bfloat16
F32 = jnp.float32


def in_vmem(value):
    return pltpu.with_memory_space_constraint(value, pltpu.VMEM)


def first_product(block_rows, block_cols, counts, start, tiles, row_blocks, cut):
    slots, size, _ = tiles.shape
    col_blocks, rank = start.shape[0] // size, start.shape[1]
    width = rank // 8

    def body(rows_ref, cols_ref, count_ref, start_hbm, tile_hbm, keep_ref, send_ref, head_ref, tail_ref, start_ref, flipped, acc, sems):
        copies = [
            pltpu.make_async_copy(start_hbm, start_ref, sems.at[0]),
            pltpu.make_async_copy(tile_hbm.at[pl.ds(0, cut)], head_ref, sems.at[1]),
            pltpu.make_async_copy(tile_hbm.at[pl.ds(cut, slots - cut)], tail_ref, sems.at[2]),
        ]
        for copy in copies:
            copy.start()
        acc[...] = jnp.zeros_like(acc)
        copies[0].wait()
        for c in range(col_blocks):
            flipped[c] = start_ref[c * size:(c + 1) * size, :].T
        copies[1].wait()
        copies[2].wait()
        count = count_ref[0, 0]
        for s in range(slots):
            to = jnp.where(s < count, rows_ref[0, s], row_blocks)
            block = head_ref[s] if s < cut else tail_ref[s - cut]
            acc[to] += lax.dot_general(
                flipped[cols_ref[0, s]], block, (((1,), (1,)), ((), ())), preferred_element_type=F32)
        x = lax.axis_index("row") % 2
        z = (lax.axis_index("col") // 2) % 2
        core = lax.axis_index("col") % 2
        for dx in range(2):
            for dz in range(2):
                at = 4 * jnp.bitwise_xor(x, dx) + 2 * jnp.bitwise_xor(z, dz)
                for ref, mine in ((keep_ref, core), (send_ref, 1 - core)):
                    first = pl.multiple_of((at + mine) * width, width)
                    ref[2 * dx + dz] = acc[0:row_blocks, pl.ds(first, width), :].astype(BF)

    smem = pl.BlockSpec(memory_space=pltpu.SMEM)
    hbm = pl.BlockSpec(memory_space=pltpu.HBM)
    vmem = pl.BlockSpec(memory_space=pltpu.VMEM)
    return pl.pallas_call(
        body,
        out_shape=[pltpu.VMEM((4, row_blocks, width, size), BF)] * 2
        + [pltpu.VMEM((n, size, size), BF) for n in (cut, slots - cut)],
        in_specs=[smem, smem, smem, hbm, hbm],
        out_specs=[vmem] * 4,
        scratch_shapes=[
            pltpu.VMEM(start.shape, BF),
            pltpu.VMEM((col_blocks, rank, size), BF),
            pltpu.VMEM((row_blocks + 1, rank, size), F32),
            pltpu.SemaphoreType.DMA((3,)),
        ],
        compiler_params=pltpu.CompilerParams(vmem_limit_bytes=12 * 1024 * 1024),
        name="first",
    )(block_rows, block_cols, counts, *[pltpu.with_memory_space_constraint(v, pltpu.HBM) for v in (start, tiles)])


def flip_blocks(tiles):
    count = len(tiles)

    def body(*refs):
        for ref, out, same in zip(refs[:count], refs[count:2 * count], refs[2 * count:]):
            def some(i, carry, ref=ref, out=out, same=same):
                block = ref[i]
                out[i] = block.T
                same[i] = block
                return carry

            n = ref.shape[0]
            lax.fori_loop(0, n, some, 0, unroll=max(u for u in range(1, 11) if n % u == 0))

    vmem = pl.BlockSpec(memory_space=pltpu.VMEM)
    out = pl.pallas_call(
        body,
        out_shape=[pltpu.VMEM(t.shape, t.dtype) for t in (*tiles, *tiles)],
        in_specs=[vmem] * count,
        out_specs=[vmem] * (2 * count),
        compiler_params=pltpu.CompilerParams(vmem_limit_bytes=8 * 1024 * 1024),
        name="flip",
    )(*[in_vmem(t) for t in tiles])
    return out[:count], out[count:]


def block_product(backward, found, groups, parts, row_blocks, col_blocks, scale_parts=(), total=None, want_sum=False,
                  want_value=False, so_far=None, want_acc=False):
    size = groups[0][0].shape[1]
    in_blocks, width, _ = parts[0].shape
    out_blocks = 4 * col_blocks if backward else 2 * row_blocks
    tiles = [g[0] for g in groups]
    n_found, n_tiles, n_parts, n_scale = len(found), len(tiles), len(parts), len(scale_parts)
    n_so_far = 0 if so_far is None else 1
    contract = (((1,), (0,)), ((), ()))

    def body(*refs):
        rest = list(refs)

        def take(count):
            out = rest[:count]
            del rest[:count]
            return out

        found_refs, tile_refs, part_refs = take(n_found), take(n_tiles), take(n_parts)
        scale_refs, so_far_refs = take(n_scale), take(n_so_far)
        (out_ref,) = take(1)
        sum_refs, value_refs = take(int(want_sum)), take(int(want_value))
        operand, acc = take(2)
        where, (sems,) = take(n_found), take(1)
        if want_acc:
            acc = out_ref
        copies = [
            pltpu.make_async_copy(found_refs[i], where[i], sems.at[i]) for i in range(n_found)]
        for copy in copies:
            copy.start()
        acc[...] = so_far_refs[0][...] if n_so_far else jnp.zeros_like(acc)
        if n_scale:
            squares = scale_refs[0][...]
            for ref in scale_refs[1:]:
                squares = squares + ref[...]
            scale = lax.rsqrt(jnp.sum(squares, axis=1, keepdims=True) / total + 1e-6)

        def gather_operand(i, carry):
            value = part_refs[0][i].astype(F32)
            for ref in part_refs[1:]:
                value = value + ref[i].astype(F32)
            if n_scale:
                value = value * scale
            operand[i] = value.astype(BF)
            if want_value:
                value_refs[0][i] = value.astype(BF)
            return carry + value * value if want_sum else carry

        squares_out = lax.fori_loop(
            0, in_blocks, gather_operand, jnp.zeros((width, size), F32) if want_sum else 0, unroll=4)
        if want_sum:
            sum_refs[0][...] = squares_out
        for copy in copies:
            copy.wait()
        for ref, (_, which, dx, dz, dc, first) in zip(tile_refs, groups):
            for s in range(ref.shape[0]):
                at_row = where[which][dc, 0, first + s]
                at_col = where[which][dc, 1, first + s] + (2 * dz + dc) * col_blocks
                live = at_row >= 0
                if backward:
                    to = jnp.where(live, at_col, out_blocks)
                    source = jnp.maximum(at_row, 0) + dx * row_blocks
                else:
                    to = jnp.where(live, at_row + dx * row_blocks, out_blocks)
                    source = at_col
                acc[to] += lax.dot_general(operand[source], ref[s], contract, preferred_element_type=F32)
        if not want_acc:
            out_ref[...] = acc[0:out_blocks].astype(BF)

    acc_shape = (out_blocks + 1, width, size)
    out_shape = [pltpu.VMEM(acc_shape, F32) if want_acc else pltpu.VMEM((out_blocks, width, size), BF)]
    if want_sum:
        out_shape.append(pltpu.VMEM((width, size), F32))
    if want_value:
        out_shape.append(pltpu.VMEM((in_blocks, width, size), BF))
    vmem = pl.BlockSpec(memory_space=pltpu.VMEM)
    others = [*tiles, *parts, *scale_parts] + ([so_far] if n_so_far else [])
    return pl.pallas_call(
        body,
        out_shape=out_shape,
        in_specs=[pl.BlockSpec(memory_space=pl.ANY)] * n_found + [vmem] * len(others),
        out_specs=[vmem] * len(out_shape),
        scratch_shapes=[
            pltpu.VMEM((in_blocks, width, size), BF),
            pltpu.VMEM((8, 128) if want_acc else acc_shape, F32),
        ]
        + [pltpu.SMEM(f.shape, jnp.int32) for f in found]
        + [pltpu.SemaphoreType.DMA((n_found,))],
        compiler_params=pltpu.CompilerParams(vmem_limit_bytes=8 * 1024 * 1024),
        name="product",
    )(*found, *[in_vmem(t) for t in others])


def assemble(messages, spans):
    _, blocks, width, size = messages[0][0].shape
    flat = [messages[dx][dz] for dx in range(2) for dz in range(2)]

    def body(*refs):
        image_ref, basis_ref, scratch = refs[4:]
        x = lax.axis_index("row") % 2
        z = (lax.axis_index("col") // 2) % 2
        core = lax.axis_index("col") % 2
        for dx in range(2):
            for dz in range(2):
                for dc in range(2):
                    at = 4 * jnp.bitwise_xor(x, dx) + 2 * jnp.bitwise_xor(z, dz) + jnp.bitwise_xor(core, dc)
                    at = pl.multiple_of(at * width, width)
                    for b in range(blocks):
                        scratch[b, pl.ds(at, width), :] = refs[2 * dx + dz][dc, b].astype(F32)
        for b in range(blocks):
            ref, row = (image_ref, b) if b < spans[0] else (basis_ref, b - spans[0])
            ref[row * size:(row + 1) * size, :] = scratch[b].T.astype(BF)

    vmem = pl.BlockSpec(memory_space=pltpu.VMEM)
    return pl.pallas_call(
        body,
        out_shape=[jax.ShapeDtypeStruct((span * size, 8 * width), BF) for span in spans],
        in_specs=[vmem] * 4,
        out_specs=[vmem] * 2,
        scratch_shapes=[pltpu.VMEM((blocks, 8 * width, size), F32)],
        compiler_params=pltpu.CompilerParams(vmem_limit_bytes=8 * 1024 * 1024),
        name="assemble",
    )(*[in_vmem(m) for m in flat])


def shards(n_row, n_col, slab_rows, block_tiles, block_rows, block_cols, counts, start_basis):
    tiles = block_tiles[0]
    slots, size, _ = tiles.shape
    slab_cols, rank = start_basis.shape
    row_blocks = slab_rows // size
    col_blocks = slab_cols // size
    width = rank // 8
    row = lax.axis_index("row")
    col = lax.axis_index("col")
    x = row % 2
    z = (col // 2) % 2
    core = col % 2
    half_z = col // 4
    half_row = row // 2

    def send(value, dx, dz, dc):
        return lax.ppermute(value, ("row", "col"), [
            (r * n_col + c, (r ^ dx) * n_col + (c ^ (2 * dz + dc)))
            for r in range(n_row) for c in range(n_col)])

    def others_z(value):
        return [
            lax.ppermute(value, "col", [(c, (c + 4 * k) % n_col) for c in range(n_col)])
            for k in range(1, n_col // 4)
        ]

    def others_row(value):
        return [
            lax.ppermute(value, "row", [(r, (r + 2 * k) % n_row) for r in range(n_row)])
            for k in range(1, n_row // 2)
        ]

    cut = slots // 2
    late = slots - slots // 5
    keep, other, tiles_0, tiles_1 = first_product(
        block_rows, block_cols, counts, start_basis, tiles, row_blocks, cut)
    image = keep.astype(F32) + send(other, 0, 0, 1).astype(F32)
    image = image.astype(BF).reshape(2, 2, row_blocks, width, size)
    image = (image[:, 0].astype(F32) + send(image[:, 1], 0, 1, 0).astype(F32)).astype(BF)
    image = jnp.concatenate([image[0], send(image[1], 1, 0, 0)])
    image = [image] + others_z(image)

    tiles_x0 = send(tiles_0, 1, 0, 0)
    tiles_x1 = send(tiles_1, 1, 0, 0)
    tiles_z0 = send(tiles_0, 0, 1, 0)
    tiles_z1 = send(tiles_1, 0, 1, 0)
    corner_0 = send(tiles_z0, 1, 0, 0)
    corner_1 = send(tiles_z1[:late - cut], 1, 0, 0)
    corner_2 = send(tiles_x1[late - cut:], 0, 1, 0)

    block_rows, block_cols, counts, _ = lax.optimization_barrier((block_rows, block_cols, counts, other))
    own = jnp.stack([
        jnp.where(jnp.arange(slots, dtype=jnp.int32) < counts[0, 0], block_rows[0], -1), block_cols[0]])
    own = jnp.stack([own, send(own, 0, 0, 1)])
    found = [own, send(own, 1, 0, 0), send(own, 0, 1, 0), send(own, 1, 1, 0)]

    groups = []
    for blocks, which, dx, dz, at in (
        (tiles_0, 0, 0, 0, 0), (tiles_1, 0, 0, 0, cut), (tiles_x0, 1, 1, 0, 0),
        (tiles_x1, 1, 1, 0, cut),
        (tiles_z0, 2, 0, 1, 0), (tiles_z1, 2, 0, 1, cut), (corner_0, 3, 1, 1, 0),
        (corner_1, 3, 1, 1, cut), (corner_2, 3, 1, 1, late)):
        groups += [(blocks, which, dx, dz, 0, at), (send(blocks, 0, 0, 1), which, dx, dz, 1, at)]

    total = n_col * slab_cols
    product = functools.partial(block_product, row_blocks=row_blocks, col_blocks=col_blocks)
    (some,) = product(True, found[:3], groups[:12], image, want_acc=True)
    (basis,) = product(True, found[3:], [(g[0], 0, *g[2:]) for g in groups[12:]], image, so_far=some)
    basis = [basis] + others_row(basis)
    flipped, same = flip_blocks([g[0] for g in groups])
    flipped = [(t, *g[1:]) for t, g in zip(flipped, groups)]
    groups = [(t, *g[1:]) for t, g in zip(same, groups)]
    image, squares = product(False, found, flipped, basis, want_sum=True)
    basis, value = product(
        True, found, groups, [image] + others_z(image),
        scale_parts=[squares] + others_z(squares), total=total, want_value=True)
    basis = [basis] + others_row(basis)
    basis = functools.reduce(jnp.add, [b.astype(F32) for b in basis])
    squares = jnp.sum(jnp.sum(basis * basis, axis=0), axis=1, keepdims=True)
    squares = functools.reduce(jnp.add, [squares] + others_z(squares))
    basis = (basis * lax.rsqrt(squares / total + 1e-6)).astype(BF)

    image_rows = slab_rows // n_col
    basis_rows = slab_cols // n_row
    image_span = max(image_rows // size, 1)
    basis_span = max(basis_rows // size, 1)
    value = value.reshape(2, row_blocks, width, size)
    basis = basis.reshape(2, 2, col_blocks, width, size)

    def pieces(dc):
        out = []
        for dx in range(2):
            for dz in range(2):
                first = (4 * half_z + 2 * (z ^ dz) + (core ^ dc)) * image_rows // size
                out.append(lax.dynamic_slice_in_dim(value[dx], first, image_span, 0))
                first = (2 * half_row + (x ^ dx)) * basis_rows // size
                out.append(lax.dynamic_slice_in_dim(basis[dz, dc], first, basis_span, 0))
        return jnp.concatenate(out).reshape(2, 2, image_span + basis_span, width, size)

    keep = pieces(0)
    twin = send(pieces(1), 0, 0, 1)
    messages = [[jnp.stack([keep[dx, dz], twin[dx, dz]]) for dz in range(2)] for dx in range(2)]
    messages = [
        [messages[0][0], send(messages[0][1], 0, 1, 0)],
        [send(messages[1][0], 1, 0, 0), send(messages[1][1], 1, 1, 0)],
    ]
    image_piece, basis_piece = assemble(messages, (image_span, basis_span))
    if image_rows < size:
        image_piece = lax.dynamic_slice_in_dim(image_piece, col * image_rows % size, image_rows, 0)
    if basis_rows < size:
        basis_piece = lax.dynamic_slice_in_dim(basis_piece, row * basis_rows % size, basis_rows, 0)
    return image_piece, basis_piece


def solution(mesh):
    n_row, n_col = mesh.shape["row"], mesh.shape["col"]

    def whole(block_tiles, block_rows, block_cols, counts, start_basis):
        slab_rows = start_basis.shape[0] // n_row
        return jax.shard_map(
            functools.partial(shards, n_row, n_col, slab_rows),
            mesh=mesh,
            in_specs=(
                P("row", "col", None, None),
                P("row", "col"),
                P("row", "col"),
                P("row", "col"),
                P("col", None),
            ),
            out_specs=(P(("row", "col"), None), P(("col", "row"), None)),
            check_vma=False,
        )(block_tiles, block_rows, block_cols, counts, start_basis)

    return whole
```

```python
import functools

import jax
import jax.numpy as jnp
from jax import lax
from jax.experimental import pallas as pl
from jax.experimental.pallas import tpu as pltpu
from jax.sharding import PartitionSpec as P


BF = jnp.bfloat16
F32 = jnp.float32


def in_vmem(value):
    return pltpu.with_memory_space_constraint(value, pltpu.VMEM)


def first_product(block_rows, block_cols, counts, start, tiles, row_blocks, cut):
    slots, size, _ = tiles.shape
    col_blocks, rank = start.shape[0] // size, start.shape[1]
    width = rank // 8

    def body(rows_ref, cols_ref, count_ref, start_hbm, tile_hbm, keep_ref, send_ref, head_ref, tail_ref, start_ref, flipped, acc, sems):
        copies = [
            pltpu.make_async_copy(start_hbm, start_ref, sems.at[0]),
            pltpu.make_async_copy(tile_hbm.at[pl.ds(0, cut)], head_ref, sems.at[1]),
            pltpu.make_async_copy(tile_hbm.at[pl.ds(cut, slots - cut)], tail_ref, sems.at[2]),
        ]
        for copy in copies:
            copy.start()
        acc[...] = jnp.zeros_like(acc)
        copies[0].wait()
        for c in range(col_blocks):
            flipped[c] = start_ref[c * size:(c + 1) * size, :].T
        copies[1].wait()
        copies[2].wait()
        count = count_ref[0, 0]
        for s in range(slots):
            to = jnp.where(s < count, rows_ref[0, s], row_blocks)
            block = head_ref[s] if s < cut else tail_ref[s - cut]
            acc[to] += lax.dot_general(
                flipped[cols_ref[0, s]], block, (((1,), (1,)), ((), ())), preferred_element_type=F32)
        x = lax.axis_index("row") % 2
        z = (lax.axis_index("col") // 2) % 2
        core = lax.axis_index("col") % 2
        for dx in range(2):
            for dz in range(2):
                at = 4 * jnp.bitwise_xor(x, dx) + 2 * jnp.bitwise_xor(z, dz)
                for ref, mine in ((keep_ref, core), (send_ref, 1 - core)):
                    first = pl.multiple_of((at + mine) * width, width)
                    ref[2 * dx + dz] = acc[0:row_blocks, pl.ds(first, width), :].astype(BF)

    smem = pl.BlockSpec(memory_space=pltpu.SMEM)
    hbm = pl.BlockSpec(memory_space=pltpu.HBM)
    vmem = pl.BlockSpec(memory_space=pltpu.VMEM)
    return pl.pallas_call(
        body,
        out_shape=[pltpu.VMEM((4, row_blocks, width, size), BF)] * 2
        + [pltpu.VMEM((n, size, size), BF) for n in (cut, slots - cut)],
        in_specs=[smem, smem, smem, hbm, hbm],
        out_specs=[vmem] * 4,
        scratch_shapes=[
            pltpu.VMEM(start.shape, BF),
            pltpu.VMEM((col_blocks, rank, size), BF),
            pltpu.VMEM((row_blocks + 1, rank, size), F32),
            pltpu.SemaphoreType.DMA((3,)),
        ],
        compiler_params=pltpu.CompilerParams(vmem_limit_bytes=12 * 1024 * 1024),
        name="first",
    )(block_rows, block_cols, counts, *[pltpu.with_memory_space_constraint(v, pltpu.HBM) for v in (start, tiles)])


def flip_blocks(tiles):
    count = len(tiles)
    size = tiles[0].shape[1]
    slots = sum(t.shape[0] for t in tiles)

    def body(*refs):
        out = refs[count]
        at = 0
        for ref in refs[:count]:
            def some(i, carry, ref=ref, at=at):
                block = ref[i]
                out[at + i] = block.T
                out[slots + at + i] = block
                return carry

            n = ref.shape[0]
            lax.fori_loop(0, n, some, 0, unroll=max(u for u in range(1, 11) if n % u == 0))
            at += n

    vmem = pl.BlockSpec(memory_space=pltpu.VMEM)
    return pl.pallas_call(
        body,
        out_shape=pltpu.VMEM((2 * slots, size, size), tiles[0].dtype),
        in_specs=[vmem] * count,
        out_specs=vmem,
        compiler_params=pltpu.CompilerParams(vmem_limit_bytes=8 * 1024 * 1024),
        name="flip",
    )(*[in_vmem(t) for t in tiles])


def block_product(backward, found, tiles, groups, parts, row_blocks, col_blocks, total=None, want_sum=False,
                  want_value=False, so_far=None, want_acc=False, split=1, skip=0):
    _, width, size = parts[0].shape
    in_blocks = 2 * row_blocks if backward else 4 * col_blocks
    out_blocks = 4 * col_blocks if backward else 2 * row_blocks
    n_found, n_tiles, n_parts = len(found), len(tiles), len(parts)
    n_so_far = 0 if so_far is None else 1
    contract = (((1,), (0,)), ((), ()))

    def body(*refs):
        rest = list(refs)

        def take(count):
            out = rest[:count]
            del rest[:count]
            return out

        found_refs, tile_refs, part_refs, so_far_refs = take(n_found), take(n_tiles), take(n_parts), take(n_so_far)
        out_refs, value_refs = take(split), take(int(want_value))
        operand, acc = take(2)
        where, (sems,) = take(n_found), take(1)
        if want_acc:
            acc = out_refs[0]
        copies = [
            pltpu.make_async_copy(found_refs[i], where[i], sems.at[i]) for i in range(n_found)]
        for copy in copies:
            copy.start()
        acc[...] = so_far_refs[0][...] if n_so_far else jnp.zeros_like(acc)
        if total is not None:
            squares = part_refs[0][in_blocks].astype(F32)
            for ref in part_refs[1:]:
                squares = squares + ref[in_blocks].astype(F32)
            scale = lax.rsqrt(jnp.sum(squares, axis=1, keepdims=True) / total + 1e-6)

        def gather_operand(i, carry):
            value = part_refs[0][i].astype(F32)
            for ref in part_refs[1:]:
                value = value + ref[i].astype(F32)
            if total is not None:
                value = value * scale
            operand[i] = value.astype(BF)
            if want_value:
                value_refs[0][i] = value.astype(BF)
            return carry + value * value if want_sum else carry

        squares = lax.fori_loop(
            0, in_blocks, gather_operand, jnp.zeros((width, size), F32) if want_sum else 0, unroll=4)
        if want_sum:
            left = jnp.broadcast_to(jnp.sum(squares, axis=1, keepdims=True), (width, size))
            lane = lax.broadcasted_iota(jnp.int32, (width, size), 1)
            term = jnp.zeros((width, size), F32)
            for k in range(3):
                rounded = left.astype(BF).astype(F32)
                term = jnp.where(lane == k, rounded, term)
                left = left - rounded
            out_refs[0][out_blocks] = term.astype(BF)
        for copy in copies:
            copy.wait()
        blocks = [(ref, i) for ref in tile_refs for i in range(ref.shape[0])][skip:]
        for count, which, dx, dz, dc, first in groups:
            for s in range(count):
                ref, i = blocks.pop(0)
                at_row = where[which][dc, 0, first + s]
                at_col = where[which][dc, 1, first + s] + (2 * dz + dc) * col_blocks
                live = at_row >= 0
                if backward:
                    to = jnp.where(live, at_col, out_blocks)
                    source = jnp.maximum(at_row, 0) + dx * row_blocks
                else:
                    to = jnp.where(live, at_row + dx * row_blocks, out_blocks)
                    source = at_col
                acc[to] += lax.dot_general(operand[source], ref[i], contract, preferred_element_type=F32)
        if not want_acc:
            part = width // split
            for k, ref in enumerate(out_refs):
                ref[0:out_blocks] = acc[0:out_blocks, k * part:(k + 1) * part, :].astype(BF)

    acc_shape = (out_blocks + 1, width, size)
    if want_acc:
        out_shape = [pltpu.VMEM(acc_shape, F32)]
    else:
        out_shape = [pltpu.VMEM((out_blocks + int(want_sum), width // split, size), BF)] * split
    if want_value:
        out_shape.append(pltpu.VMEM((in_blocks, width, size), BF))
    vmem = pl.BlockSpec(memory_space=pltpu.VMEM)
    others = [*tiles, *parts] + ([so_far] if n_so_far else [])
    return pl.pallas_call(
        body,
        out_shape=out_shape,
        in_specs=[pl.BlockSpec(memory_space=pl.ANY)] * n_found + [vmem] * len(others),
        out_specs=[vmem] * len(out_shape),
        scratch_shapes=[
            pltpu.VMEM((in_blocks, width, size), BF),
            pltpu.VMEM((8, 128) if want_acc else acc_shape, F32),
        ]
        + [pltpu.SMEM(f.shape, jnp.int32) for f in found]
        + [pltpu.SemaphoreType.DMA((n_found,))],
        compiler_params=pltpu.CompilerParams(vmem_limit_bytes=8 * 1024 * 1024),
        name="product",
    )(*found, *[in_vmem(t) for t in others])


def pack(values, basis, spans, rows, row_blocks, col_blocks):
    count = len(values)
    terms = len(basis[0])
    _, part, size = values[0].shape
    width = part * count

    def body(*refs):
        value_refs = refs[:count]
        basis_refs = [refs[count + terms * k:count + terms * (k + 1)] for k in range(count)]
        keep_ref, other_ref, squares_ref, summed = refs[count * (terms + 1):]
        row, col = lax.axis_index("row"), lax.axis_index("col")
        x, z, core = row % 2, (col // 2) % 2, col % 2
        for k in range(count):
            def add(i, carry, k=k):
                value = basis_refs[k][0][i].astype(F32)
                for ref in basis_refs[k][1:]:
                    value = value + ref[i].astype(F32)
                summed[i, k * part:(k + 1) * part, :] = value
                return carry + value * value

            squares = lax.fori_loop(0, 4 * col_blocks, add, jnp.zeros((part, size), F32), unroll=4)
            squares_ref[k * part:(k + 1) * part, :] = squares
        for dx in range(2):
            for dz in range(2):
                for dc, ref in ((0, keep_ref), (1, other_ref)):
                    at = 4 * (col // 4) + 2 * jnp.bitwise_xor(z, dz) + jnp.bitwise_xor(core, dc)
                    first = dx * row_blocks + at * rows[0] // size
                    for b in range(spans[0]):
                        for k in range(count):
                            ref[dx, dz, b, k * part:(k + 1) * part, :] = value_refs[k][first + b]
                    at = 2 * (row // 2) + jnp.bitwise_xor(x, dx)
                    first = (2 * dz + dc) * col_blocks + at * rows[1] // size
                    for b in range(spans[1]):
                        ref[dx, dz, spans[0] + b] = summed[first + b].astype(BF)

    vmem = pl.BlockSpec(memory_space=pltpu.VMEM)
    operands = [*values, *[t for b in basis for t in b]]
    return pl.pallas_call(
        body,
        out_shape=[pltpu.VMEM((2, 2, sum(spans), width, size), BF)] * 2 + [pltpu.VMEM((width, size), F32)],
        in_specs=[vmem] * len(operands),
        out_specs=[vmem] * 3,
        scratch_shapes=[pltpu.VMEM((4 * col_blocks, width, size), F32)],
        compiler_params=pltpu.CompilerParams(vmem_limit_bytes=8 * 1024 * 1024),
        name="pack",
    )(*[in_vmem(t) for t in operands])


def assemble(messages, spans):
    _, blocks, width, size = messages[0][0].shape
    flat = [messages[dx][dz] for dx in range(2) for dz in range(2)]

    def body(*refs):
        image_ref, basis_ref, scratch = refs[4:]
        x = lax.axis_index("row") % 2
        z = (lax.axis_index("col") // 2) % 2
        core = lax.axis_index("col") % 2
        for dx in range(2):
            for dz in range(2):
                for dc in range(2):
                    at = 4 * jnp.bitwise_xor(x, dx) + 2 * jnp.bitwise_xor(z, dz) + jnp.bitwise_xor(core, dc)
                    at = pl.multiple_of(at * width, width)
                    for b in range(blocks):
                        scratch[b, pl.ds(at, width), :] = refs[2 * dx + dz][dc, b].astype(F32)
        for b in range(blocks):
            ref, row = (image_ref, b) if b < spans[0] else (basis_ref, b - spans[0])
            ref[row * size:(row + 1) * size, :] = scratch[b].T.astype(BF)

    vmem = pl.BlockSpec(memory_space=pltpu.VMEM)
    return pl.pallas_call(
        body,
        out_shape=[jax.ShapeDtypeStruct((span * size, 8 * width), BF) for span in spans],
        in_specs=[vmem] * 4,
        out_specs=[vmem] * 2,
        scratch_shapes=[pltpu.VMEM((blocks, 8 * width, size), F32)],
        compiler_params=pltpu.CompilerParams(vmem_limit_bytes=8 * 1024 * 1024),
        name="assemble",
    )(*[in_vmem(m) for m in flat])


def shards(n_row, n_col, slab_rows, block_tiles, block_rows, block_cols, counts, start_basis):
    tiles = block_tiles[0]
    slots, size, _ = tiles.shape
    slab_cols, rank = start_basis.shape
    row_blocks = slab_rows // size
    col_blocks = slab_cols // size
    width = rank // 8

    def send(value, dx, dz, dc):
        return lax.ppermute(value, ("row", "col"), [
            (r * n_col + c, (r ^ dx) * n_col + (c ^ (2 * dz + dc)))
            for r in range(n_row) for c in range(n_col)])

    def others_z(value):
        return [
            lax.ppermute(value, "col", [(c, (c + 4 * k) % n_col) for c in range(n_col)])
            for k in range(1, n_col // 4)
        ]

    def others_row(value):
        return [
            lax.ppermute(value, "row", [(r, (r + 2 * k) % n_row) for r in range(n_row)])
            for k in range(1, n_row // 2)
        ]

    cut = slots // 2
    late = slots - slots // 5
    keep, other, tiles_0, tiles_1 = first_product(
        block_rows, block_cols, counts, start_basis, tiles, row_blocks, cut)
    image = keep.astype(F32) + send(other, 0, 0, 1).astype(F32)
    image = image.astype(BF).reshape(2, 2, row_blocks, width, size)
    image = (image[:, 0].astype(F32) + send(image[:, 1], 0, 1, 0).astype(F32)).astype(BF)
    image = jnp.concatenate([image[0], send(image[1], 1, 0, 0)])
    image = [image] + others_z(image)

    tiles_x0 = send(tiles_0, 1, 0, 0)
    tiles_x1 = send(tiles_1, 1, 0, 0)
    tiles_z0 = send(tiles_0, 0, 1, 0)
    tiles_z1 = send(tiles_1, 0, 1, 0)
    corner_0 = send(tiles_z0, 1, 0, 0)
    corner_1 = send(tiles_z1[:late - cut], 1, 0, 0)
    corner_2 = send(tiles_x1[late - cut:], 0, 1, 0)

    block_rows, block_cols, counts, _ = lax.optimization_barrier((block_rows, block_cols, counts, other))
    own = jnp.stack([
        jnp.where(jnp.arange(slots, dtype=jnp.int32) < counts[0, 0], block_rows[0], -1), block_cols[0]])
    own = jnp.stack([own, send(own, 0, 0, 1)])
    found = [own, send(own, 1, 0, 0), send(own, 0, 1, 0), send(own, 1, 1, 0)]

    blocks, groups = [], []
    for some, which, dx, dz, at in (
        (tiles_0, 0, 0, 0, 0), (tiles_1, 0, 0, 0, cut), (tiles_x0, 1, 1, 0, 0),
        (tiles_x1, 1, 1, 0, cut), (tiles_z0, 2, 0, 1, 0), (tiles_z1, 2, 0, 1, cut),
        (corner_0, 3, 1, 1, 0), (corner_1, 3, 1, 1, cut), (corner_2, 3, 1, 1, late)):
        blocks += [some, send(some, 0, 0, 1)]
        groups += [(some.shape[0], which, dx, dz, dc, at) for dc in range(2)]

    total = n_col * slab_cols
    product = functools.partial(block_product, row_blocks=row_blocks, col_blocks=col_blocks)
    (near,) = product(True, found[:3], blocks[:12], groups[:12], image, want_acc=True)
    corner = [(g[0], 0, *g[2:]) for g in groups[12:]]
    basis = product(True, found[3:], blocks[12:], corner, image, so_far=near, split=2)
    both = flip_blocks(blocks)
    as_they_are = both.shape[0] // 2

    basis = [[b] + others_row(b) for b in basis]
    image = []
    for b in basis:
        (out,) = product(False, found, [both], groups, b, want_sum=True)
        image.append([out] + others_z(out))
    basis, values = [], []
    for i in image:
        out, value = product(True, found, [both], groups, i, total=total, want_value=True, skip=as_they_are)
        values.append(value)
        basis.append([out] + others_row(out))
    image_rows = slab_rows // n_col
    basis_rows = slab_cols // n_row
    image_span = max(image_rows // size, 1)
    basis_span = max(basis_rows // size, 1)
    keep, other, squares = pack(
        values, basis, (image_span, basis_span), (image_rows, basis_rows), row_blocks, col_blocks)

    twin_squares = [
        lax.ppermute(squares, "col", [(c, (c + 4 * k) % n_col ^ 1) for c in range(n_col)])
        for k in range(1, n_col // 4)
    ]
    twin_squares = functools.reduce(jnp.add, twin_squares + [send(squares, 0, 0, 1)])
    squares = functools.reduce(jnp.add, [squares] + others_z(squares))

    twin = send(other, 0, 0, 1)

    def scaled(piece, sums):
        factor = lax.rsqrt(jnp.sum(sums, axis=1, keepdims=True) / total + 1e-6)
        factor = jnp.broadcast_to(factor, (basis_span, width, 1))
        factor = jnp.concatenate([jnp.ones((image_span, width, 1), F32), factor])
        return (piece.astype(F32) * factor).astype(BF)

    messages = [[jnp.stack([scaled(keep[dx, dz], squares), scaled(twin[dx, dz], twin_squares)]) for dz in range(2)] for dx in range(2)]
    messages = [
        [messages[0][0], send(messages[0][1], 0, 1, 0)],
        [send(messages[1][0], 1, 0, 0), send(messages[1][1], 1, 1, 0)],
    ]
    image_piece, basis_piece = assemble(messages, (image_span, basis_span))
    if image_rows < size:
        image_piece = lax.dynamic_slice_in_dim(image_piece, lax.axis_index("col") * image_rows % size, image_rows, 0)
    if basis_rows < size:
        basis_piece = lax.dynamic_slice_in_dim(basis_piece, lax.axis_index("row") * basis_rows % size, basis_rows, 0)
    return image_piece, basis_piece


def solution(mesh):
    n_row, n_col = mesh.shape["row"], mesh.shape["col"]

    def whole(block_tiles, block_rows, block_cols, counts, start_basis):
        slab_rows = start_basis.shape[0] // n_row
        return jax.shard_map(
            functools.partial(shards, n_row, n_col, slab_rows),
            mesh=mesh,
            in_specs=(
                P("row", "col", None, None),
                P("row", "col"),
                P("row", "col"),
                P("row", "col"),
                P("col", None),
            ),
            out_specs=(P(("row", "col"), None), P(("col", "row"), None)),
            check_vma=False,
        )(block_tiles, block_rows, block_cols, counts, start_basis)

    return whole
```

```python
import functools

import jax
import jax.numpy as jnp
from jax import lax
from jax.experimental import pallas as pl
from jax.experimental.pallas import tpu as pltpu
from jax.sharding import PartitionSpec as P


BF = jnp.bfloat16
F32 = jnp.float32


def in_vmem(value):
    return pltpu.with_memory_space_constraint(value, pltpu.VMEM)


def in_hbm(value):
    return pltpu.with_memory_space_constraint(value, pltpu.HBM)


def first_product(block_rows, block_cols, counts, start, tiles, row_blocks, cut):
    slots, size, _ = tiles.shape
    col_blocks, rank = start.shape[0] // size, start.shape[1]
    width = rank // 8

    def body(rows_hbm, cols_hbm, count_ref, start_hbm, tile_hbm, keep_ref, send_ref, head_ref, tail_ref, start_ref,
             flipped, acc, rows_ref, cols_ref, sems):
        copies = [
            pltpu.make_async_copy(start_hbm, start_ref, sems.at[0]),
            pltpu.make_async_copy(tile_hbm.at[pl.ds(0, cut)], head_ref, sems.at[1]),
            pltpu.make_async_copy(tile_hbm.at[pl.ds(cut, slots - cut)], tail_ref, sems.at[2]),
            pltpu.make_async_copy(rows_hbm, rows_ref, sems.at[3]),
            pltpu.make_async_copy(cols_hbm, cols_ref, sems.at[4]),
        ]
        for copy in copies:
            copy.start()
        acc[...] = jnp.zeros_like(acc)
        copies[0].wait()
        for c in range(col_blocks):
            flipped[c] = start_ref[c * size:(c + 1) * size, :].T
        for copy in copies[1:]:
            copy.wait()
        count = count_ref[0, 0]
        for s in range(slots):
            to = jnp.where(s < count, rows_ref[0, s], row_blocks)
            block = head_ref[s] if s < cut else tail_ref[s - cut]
            acc[to] += lax.dot_general(
                flipped[cols_ref[0, s]], block, (((1,), (1,)), ((), ())), preferred_element_type=F32)
        x = lax.axis_index("row") % 2
        z = (lax.axis_index("col") // 2) % 2
        core = lax.axis_index("col") % 2
        for dx in range(2):
            for dz in range(2):
                at = 4 * jnp.bitwise_xor(x, dx) + 2 * jnp.bitwise_xor(z, dz)
                for ref, mine in ((keep_ref, core), (send_ref, 1 - core)):
                    first = pl.multiple_of((at + mine) * width, width)
                    ref[2 * dx + dz] = acc[0:row_blocks, pl.ds(first, width), :].astype(BF)

    hbm = pl.BlockSpec(memory_space=pltpu.HBM)
    vmem = pl.BlockSpec(memory_space=pltpu.VMEM)
    return pl.pallas_call(
        body,
        out_shape=[pltpu.VMEM((4, row_blocks, width, size), BF)] * 2
        + [pltpu.VMEM((n, size, size), BF) for n in (cut, slots - cut)],
        in_specs=[hbm, hbm, pl.BlockSpec(memory_space=pltpu.SMEM), hbm, hbm],
        out_specs=[vmem] * 4,
        scratch_shapes=[
            pltpu.VMEM(start.shape, BF),
            pltpu.VMEM((col_blocks, rank, size), BF),
            pltpu.VMEM((row_blocks + 1, rank, size), F32),
            pltpu.SMEM(block_rows.shape, jnp.int32),
            pltpu.SMEM(block_cols.shape, jnp.int32),
            pltpu.SemaphoreType.DMA((5,)),
        ],
        compiler_params=pltpu.CompilerParams(vmem_limit_bytes=12 * 1024 * 1024),
        name="first",
    )(in_hbm(block_rows), in_hbm(block_cols), counts, in_hbm(start), in_hbm(tiles))


def flip_blocks(tiles):
    count = len(tiles)
    size = tiles[0].shape[1]
    slots = sum(t.shape[0] for t in tiles)

    def body(*refs):
        out = refs[count]
        at = 0
        for ref in refs[:count]:
            def some(i, carry, ref=ref, at=at):
                block = ref[i]
                out[at + i] = block.T
                out[slots + at + i] = block
                return carry

            n = ref.shape[0]
            lax.fori_loop(0, n, some, 0, unroll=max(u for u in range(1, 11) if n % u == 0))
            at += n

    vmem = pl.BlockSpec(memory_space=pltpu.VMEM)
    return pl.pallas_call(
        body,
        out_shape=pltpu.VMEM((2 * slots, size, size), tiles[0].dtype),
        in_specs=[vmem] * count,
        out_specs=vmem,
        compiler_params=pltpu.CompilerParams(vmem_limit_bytes=8 * 1024 * 1024),
        name="flip",
    )(*[in_vmem(t) for t in tiles])


def block_product(backward, found, tiles, groups, parts, row_blocks, col_blocks, total=None, want_sum=False,
                  want_value=False, so_far=None, want_acc=False, split=1, skip=0):
    _, width, size = parts[0].shape
    in_blocks = 2 * row_blocks if backward else 4 * col_blocks
    out_blocks = 4 * col_blocks if backward else 2 * row_blocks
    n_found, n_tiles, n_parts = len(found), len(tiles), len(parts)
    n_so_far = 0 if so_far is None else 1
    contract = (((1,), (0,)), ((), ()))

    def body(*refs):
        rest = list(refs)

        def take(count):
            out = rest[:count]
            del rest[:count]
            return out

        found_refs, tile_refs, part_refs, so_far_refs = take(n_found), take(n_tiles), take(n_parts), take(n_so_far)
        out_refs, value_refs = take(split), take(int(want_value))
        operand, acc = take(2)
        where, (sems,) = take(n_found), take(1)
        if want_acc:
            acc = out_refs[0]
        copies = [
            pltpu.make_async_copy(found_refs[i], where[i], sems.at[i]) for i in range(n_found)]
        for copy in copies:
            copy.start()
        acc[...] = so_far_refs[0][...] if n_so_far else jnp.zeros_like(acc)
        if total is not None:
            squares = part_refs[0][in_blocks].astype(F32)
            for ref in part_refs[1:]:
                squares = squares + ref[in_blocks].astype(F32)
            scale = lax.rsqrt(jnp.sum(squares, axis=1, keepdims=True) / total + 1e-6)

        def gather_operand(i, carry):
            value = part_refs[0][i].astype(F32)
            for ref in part_refs[1:]:
                value = value + ref[i].astype(F32)
            if total is not None:
                value = value * scale
            operand[i] = value.astype(BF)
            if want_value:
                value_refs[0][i] = value.astype(BF)
            return carry + value * value if want_sum else carry

        squares = lax.fori_loop(
            0, in_blocks, gather_operand, jnp.zeros((width, size), F32) if want_sum else 0, unroll=4)
        if want_sum:
            left = jnp.broadcast_to(jnp.sum(squares, axis=1, keepdims=True), (width, size))
            lane = lax.broadcasted_iota(jnp.int32, (width, size), 1)
            term = jnp.zeros((width, size), F32)
            for k in range(3):
                rounded = left.astype(BF).astype(F32)
                term = jnp.where(lane == k, rounded, term)
                left = left - rounded
            out_refs[0][out_blocks] = term.astype(BF)
        for copy in copies:
            copy.wait()
        blocks = [(ref, i) for ref in tile_refs for i in range(ref.shape[0])][skip:]
        for count, which, dx, dz, dc, first in groups:
            for s in range(count):
                ref, i = blocks.pop(0)
                at_row = where[which][dc, 0, first + s]
                at_col = where[which][dc, 1, first + s] + (2 * dz + dc) * col_blocks
                live = at_row >= 0
                if backward:
                    to = jnp.where(live, at_col, out_blocks)
                    source = jnp.maximum(at_row, 0) + dx * row_blocks
                else:
                    to = jnp.where(live, at_row + dx * row_blocks, out_blocks)
                    source = at_col
                acc[to] += lax.dot_general(operand[source], ref[i], contract, preferred_element_type=F32)
        if not want_acc:
            part = width // split
            for k, ref in enumerate(out_refs):
                ref[0:out_blocks] = acc[0:out_blocks, k * part:(k + 1) * part, :].astype(BF)

    acc_shape = (out_blocks + 1, width, size)
    if want_acc:
        out_shape = [pltpu.VMEM(acc_shape, F32)]
    else:
        out_shape = [pltpu.VMEM((out_blocks + int(want_sum), width // split, size), BF)] * split
    if want_value:
        out_shape.append(pltpu.VMEM((in_blocks, width, size), BF))
    vmem = pl.BlockSpec(memory_space=pltpu.VMEM)
    others = [*tiles, *parts] + ([so_far] if n_so_far else [])
    return pl.pallas_call(
        body,
        out_shape=out_shape,
        in_specs=[pl.BlockSpec(memory_space=pl.ANY)] * n_found + [vmem] * len(others),
        out_specs=[vmem] * len(out_shape),
        scratch_shapes=[
            pltpu.VMEM((in_blocks, width, size), BF),
            pltpu.VMEM((8, 128) if want_acc else acc_shape, F32),
        ]
        + [pltpu.SMEM(f.shape, jnp.int32) for f in found]
        + [pltpu.SemaphoreType.DMA((n_found,))],
        compiler_params=pltpu.CompilerParams(vmem_limit_bytes=8 * 1024 * 1024),
        name="product",
    )(*found, *[in_vmem(t) for t in others])


def pack(values, basis, spans, rows, row_blocks, col_blocks):
    count = len(values)
    terms = len(basis[0])
    _, part, size = values[0].shape
    width = part * count

    def body(*refs):
        value_refs = refs[:count]
        basis_refs = [refs[count + terms * k:count + terms * (k + 1)] for k in range(count)]
        keep_ref, other_ref, squares_ref, summed = refs[count * (terms + 1):]
        row, col = lax.axis_index("row"), lax.axis_index("col")
        x, z, core = row % 2, (col // 2) % 2, col % 2
        for k in range(count):
            def add(i, carry, k=k):
                value = basis_refs[k][0][i].astype(F32)
                for ref in basis_refs[k][1:]:
                    value = value + ref[i].astype(F32)
                summed[i, k * part:(k + 1) * part, :] = value
                return carry + value * value

            squares = lax.fori_loop(0, 4 * col_blocks, add, jnp.zeros((part, size), F32), unroll=4)
            squares_ref[k * part:(k + 1) * part, :] = squares
        for dx in range(2):
            for dz in range(2):
                for dc, ref in ((0, keep_ref), (1, other_ref)):
                    at = 4 * (col // 4) + 2 * jnp.bitwise_xor(z, dz) + jnp.bitwise_xor(core, dc)
                    first = dx * row_blocks + at * rows[0] // size
                    for b in range(spans[0]):
                        for k in range(count):
                            ref[dx, dz, b, k * part:(k + 1) * part, :] = value_refs[k][first + b]
                    at = 2 * (row // 2) + jnp.bitwise_xor(x, dx)
                    first = (2 * dz + dc) * col_blocks + at * rows[1] // size
                    for b in range(spans[1]):
                        ref[dx, dz, spans[0] + b] = summed[first + b].astype(BF)

    vmem = pl.BlockSpec(memory_space=pltpu.VMEM)
    operands = [*values, *[t for b in basis for t in b]]
    return pl.pallas_call(
        body,
        out_shape=[pltpu.VMEM((2, 2, sum(spans), width, size), BF)] * 2 + [pltpu.VMEM((width, size), F32)],
        in_specs=[vmem] * len(operands),
        out_specs=[vmem] * 3,
        scratch_shapes=[pltpu.VMEM((4 * col_blocks, width, size), F32)],
        compiler_params=pltpu.CompilerParams(vmem_limit_bytes=8 * 1024 * 1024),
        name="pack",
    )(*[in_vmem(t) for t in operands])


def assemble(messages, spans):
    _, blocks, width, size = messages[0][0].shape
    flat = [messages[dx][dz] for dx in range(2) for dz in range(2)]

    def body(*refs):
        image_ref, basis_ref, scratch = refs[4:]
        x = lax.axis_index("row") % 2
        z = (lax.axis_index("col") // 2) % 2
        core = lax.axis_index("col") % 2
        for dx in range(2):
            for dz in range(2):
                for dc in range(2):
                    at = 4 * jnp.bitwise_xor(x, dx) + 2 * jnp.bitwise_xor(z, dz) + jnp.bitwise_xor(core, dc)
                    at = pl.multiple_of(at * width, width)
                    for b in range(blocks):
                        scratch[b, pl.ds(at, width), :] = refs[2 * dx + dz][dc, b].astype(F32)
        for b in range(blocks):
            ref, row = (image_ref, b) if b < spans[0] else (basis_ref, b - spans[0])
            ref[row * size:(row + 1) * size, :] = scratch[b].T.astype(BF)

    vmem = pl.BlockSpec(memory_space=pltpu.VMEM)
    return pl.pallas_call(
        body,
        out_shape=[jax.ShapeDtypeStruct((span * size, 8 * width), BF) for span in spans],
        in_specs=[vmem] * 4,
        out_specs=[vmem] * 2,
        scratch_shapes=[pltpu.VMEM((blocks, 8 * width, size), F32)],
        compiler_params=pltpu.CompilerParams(vmem_limit_bytes=8 * 1024 * 1024),
        name="assemble",
    )(*[in_vmem(m) for m in flat])


def shards(n_row, n_col, slab_rows, block_tiles, block_rows, block_cols, counts, start_basis):
    tiles = block_tiles[0]
    slots, size, _ = tiles.shape
    slab_cols, rank = start_basis.shape
    row_blocks = slab_rows // size
    col_blocks = slab_cols // size
    width = rank // 8

    def send(value, dx, dz, dc):
        return lax.ppermute(value, ("row", "col"), [
            (r * n_col + c, (r ^ dx) * n_col + (c ^ (2 * dz + dc)))
            for r in range(n_row) for c in range(n_col)])

    def others_z(value):
        return [
            lax.ppermute(value, "col", [(c, (c + 4 * k) % n_col) for c in range(n_col)])
            for k in range(1, n_col // 4)
        ]

    def others_row(value):
        return [
            lax.ppermute(value, "row", [(r, (r + 2 * k) % n_row) for r in range(n_row)])
            for k in range(1, n_row // 2)
        ]

    cut = slots // 2
    late = slots - slots // 5
    keep, other, tiles_0, tiles_1 = first_product(
        block_rows, block_cols, counts, start_basis, tiles, row_blocks, cut)
    image = keep.astype(F32) + send(other, 0, 0, 1).astype(F32)
    image = image.astype(BF).reshape(2, 2, row_blocks, width, size)
    image = (image[:, 0].astype(F32) + send(image[:, 1], 0, 1, 0).astype(F32)).astype(BF)
    image = jnp.concatenate([image[0], send(image[1], 1, 0, 0)])
    image = [image] + others_z(image)

    tiles_x0 = send(tiles_0, 1, 0, 0)
    tiles_x1 = send(tiles_1, 1, 0, 0)
    tiles_z0 = send(tiles_0, 0, 1, 0)
    tiles_z1 = send(tiles_1, 0, 1, 0)
    corner_0 = send(tiles_z0, 1, 0, 0)
    corner_1 = send(tiles_z1[:late - cut], 1, 0, 0)
    corner_2 = send(tiles_x1[late - cut:], 0, 1, 0)

    block_rows, block_cols, counts, _ = lax.optimization_barrier((block_rows, block_cols, counts, other))
    own = jnp.stack([
        jnp.where(jnp.arange(slots, dtype=jnp.int32) < counts[0, 0], block_rows[0], -1), block_cols[0]])
    own = jnp.stack([own, send(own, 0, 0, 1)])
    found = [own, send(own, 1, 0, 0), send(own, 0, 1, 0), send(own, 1, 1, 0)]

    blocks, groups = [], []
    for some, which, dx, dz, at in (
        (tiles_0, 0, 0, 0, 0), (tiles_1, 0, 0, 0, cut), (tiles_x0, 1, 1, 0, 0),
        (tiles_x1, 1, 1, 0, cut), (tiles_z0, 2, 0, 1, 0), (tiles_z1, 2, 0, 1, cut),
        (corner_0, 3, 1, 1, 0), (corner_1, 3, 1, 1, cut), (corner_2, 3, 1, 1, late)):
        blocks += [some, send(some, 0, 0, 1)]
        groups += [(some.shape[0], which, dx, dz, dc, at) for dc in range(2)]

    total = n_col * slab_cols
    product = functools.partial(block_product, row_blocks=row_blocks, col_blocks=col_blocks)
    (near,) = product(True, found[:3], blocks[:12], groups[:12], image, want_acc=True)
    corner = [(g[0], 0, *g[2:]) for g in groups[12:]]
    basis = product(True, found[3:], blocks[12:], corner, image, so_far=near, split=2)
    both = flip_blocks(blocks)
    as_they_are = both.shape[0] // 2

    basis = [[b] + others_row(b) for b in basis]
    image = []
    for b in basis:
        (out,) = product(False, found, [both], groups, b, want_sum=True)
        image.append([out] + others_z(out))
    basis, values = [], []
    for i in image:
        out, value = product(True, found, [both], groups, i, total=total, want_value=True, skip=as_they_are)
        values.append(value)
        basis.append([out] + others_row(out))
    image_rows = slab_rows // n_col
    basis_rows = slab_cols // n_row
    image_span = max(image_rows // size, 1)
    basis_span = max(basis_rows // size, 1)
    keep, other, squares = pack(
        values, basis, (image_span, basis_span), (image_rows, basis_rows), row_blocks, col_blocks)

    twin_squares = [
        lax.ppermute(squares, "col", [(c, (c + 4 * k) % n_col ^ 1) for c in range(n_col)])
        for k in range(1, n_col // 4)
    ]
    twin_squares = functools.reduce(jnp.add, twin_squares + [send(squares, 0, 0, 1)])
    squares = functools.reduce(jnp.add, [squares] + others_z(squares))

    twin = send(other, 0, 0, 1)

    def scaled(piece, sums):
        factor = lax.rsqrt(jnp.sum(sums, axis=1, keepdims=True) / total + 1e-6)
        factor = jnp.broadcast_to(factor, (basis_span, width, 1))
        factor = jnp.concatenate([jnp.ones((image_span, width, 1), F32), factor])
        return (piece.astype(F32) * factor).astype(BF)

    messages = [[jnp.stack([scaled(keep[dx, dz], squares), scaled(twin[dx, dz], twin_squares)]) for dz in range(2)] for dx in range(2)]
    messages = [
        [messages[0][0], send(messages[0][1], 0, 1, 0)],
        [send(messages[1][0], 1, 0, 0), send(messages[1][1], 1, 1, 0)],
    ]
    image_piece, basis_piece = assemble(messages, (image_span, basis_span))
    if image_rows < size:
        image_piece = lax.dynamic_slice_in_dim(image_piece, lax.axis_index("col") * image_rows % size, image_rows, 0)
    if basis_rows < size:
        basis_piece = lax.dynamic_slice_in_dim(basis_piece, lax.axis_index("row") * basis_rows % size, basis_rows, 0)
    return image_piece, basis_piece


def solution(mesh):
    n_row, n_col = mesh.shape["row"], mesh.shape["col"]

    def whole(block_tiles, block_rows, block_cols, counts, start_basis):
        slab_rows = start_basis.shape[0] // n_row
        return jax.shard_map(
            functools.partial(shards, n_row, n_col, slab_rows),
            mesh=mesh,
            in_specs=(
                P("row", "col", None, None),
                P("row", "col"),
                P("row", "col"),
                P("row", "col"),
                P("col", None),
            ),
            out_specs=(P(("row", "col"), None), P(("col", "row"), None)),
            check_vma=False,
        )(block_tiles, block_rows, block_cols, counts, start_basis)

    return whole
```

```python
import functools

import jax
import jax.numpy as jnp
from jax import lax
from jax.experimental import pallas as pl
from jax.experimental.pallas import tpu as pltpu
from jax.sharding import PartitionSpec as P


BF = jnp.bfloat16
F32 = jnp.float32


def in_vmem(value):
    return pltpu.with_memory_space_constraint(value, pltpu.VMEM)


def in_hbm(value):
    return pltpu.with_memory_space_constraint(value, pltpu.HBM)


def first_product(block_rows, block_cols, counts, start, tiles, row_blocks, cut):
    slots, size, _ = tiles.shape
    col_blocks, rank = start.shape[0] // size, start.shape[1]
    width = rank // 8

    def body(rows_hbm, cols_hbm, count_ref, start_hbm, tile_hbm, keep_ref, send_ref, head_ref, tail_ref, start_ref,
             flipped, acc, rows_ref, cols_ref, sems):
        copies = [
            pltpu.make_async_copy(start_hbm, start_ref, sems.at[0]),
            pltpu.make_async_copy(tile_hbm.at[pl.ds(0, cut)], head_ref, sems.at[1]),
            pltpu.make_async_copy(tile_hbm.at[pl.ds(cut, slots - cut)], tail_ref, sems.at[2]),
            pltpu.make_async_copy(rows_hbm, rows_ref, sems.at[3]),
            pltpu.make_async_copy(cols_hbm, cols_ref, sems.at[4]),
        ]
        for copy in copies:
            copy.start()
        acc[...] = jnp.zeros_like(acc)
        copies[0].wait()
        for c in range(col_blocks):
            flipped[c] = start_ref[c * size:(c + 1) * size, :].T
        for copy in copies[1:]:
            copy.wait()
        count = count_ref[0, 0]
        for s in range(slots):
            to = jnp.where(s < count, rows_ref[0, s], row_blocks)
            block = head_ref[s] if s < cut else tail_ref[s - cut]
            acc[to] += lax.dot_general(
                flipped[cols_ref[0, s]], block, (((1,), (1,)), ((), ())), preferred_element_type=F32)
        x = lax.axis_index("row") % 2
        z = (lax.axis_index("col") // 2) % 2
        core = lax.axis_index("col") % 2
        for dx in range(2):
            for dz in range(2):
                at = 4 * jnp.bitwise_xor(x, dx) + 2 * jnp.bitwise_xor(z, dz)
                for ref, mine in ((keep_ref, core), (send_ref, 1 - core)):
                    first = pl.multiple_of((at + mine) * width, width)
                    ref[2 * dx + dz] = acc[0:row_blocks, pl.ds(first, width), :].astype(BF)

    hbm = pl.BlockSpec(memory_space=pltpu.HBM)
    vmem = pl.BlockSpec(memory_space=pltpu.VMEM)
    return pl.pallas_call(
        body,
        out_shape=[pltpu.VMEM((4, row_blocks, width, size), BF)] * 2
        + [pltpu.VMEM((n, size, size), BF) for n in (cut, slots - cut)],
        in_specs=[hbm, hbm, pl.BlockSpec(memory_space=pltpu.SMEM), hbm, hbm],
        out_specs=[vmem] * 4,
        scratch_shapes=[
            pltpu.VMEM(start.shape, BF),
            pltpu.VMEM((col_blocks, rank, size), BF),
            pltpu.VMEM((row_blocks + 1, rank, size), F32),
            pltpu.SMEM(block_rows.shape, jnp.int32),
            pltpu.SMEM(block_cols.shape, jnp.int32),
            pltpu.SemaphoreType.DMA((5,)),
        ],
        compiler_params=pltpu.CompilerParams(vmem_limit_bytes=12 * 1024 * 1024),
        name="first",
    )(in_hbm(block_rows), in_hbm(block_cols), counts, in_hbm(start), in_hbm(tiles))


def flip_blocks(tiles):
    count = len(tiles)
    size = tiles[0].shape[1]
    slots = sum(t.shape[0] for t in tiles)

    def body(*refs):
        out = refs[count]
        at = 0
        for ref in refs[:count]:
            def some(i, carry, ref=ref, at=at):
                block = ref[i]
                out[at + i] = block.T
                out[slots + at + i] = block
                return carry

            n = ref.shape[0]
            lax.fori_loop(0, n, some, 0, unroll=max(u for u in range(1, 11) if n % u == 0))
            at += n

    vmem = pl.BlockSpec(memory_space=pltpu.VMEM)
    return pl.pallas_call(
        body,
        out_shape=pltpu.VMEM((2 * slots, size, size), tiles[0].dtype),
        in_specs=[vmem] * count,
        out_specs=vmem,
        compiler_params=pltpu.CompilerParams(vmem_limit_bytes=8 * 1024 * 1024),
        name="flip",
    )(*[in_vmem(t) for t in tiles])


def block_product(backward, found, tiles, groups, parts, row_blocks, col_blocks, total=None, want_sum=False,
                  want_value=False, so_far=None, want_acc=False, split=1, skip=0):
    _, width, size = parts[0].shape
    in_blocks = 2 * row_blocks if backward else 4 * col_blocks
    out_blocks = 4 * col_blocks if backward else 2 * row_blocks
    n_found, n_tiles, n_parts = len(found), len(tiles), len(parts)
    n_so_far = 0 if so_far is None else 1
    contract = (((1,), (0,)), ((), ()))

    def body(*refs):
        rest = list(refs)

        def take(count):
            out = rest[:count]
            del rest[:count]
            return out

        found_refs, tile_refs, part_refs, so_far_refs = take(n_found), take(n_tiles), take(n_parts), take(n_so_far)
        out_refs, value_refs = take(split), take(int(want_value))
        operand, acc = take(2)
        where, (sems,) = take(n_found), take(1)
        if want_acc:
            acc = out_refs[0]
        copies = [
            pltpu.make_async_copy(found_refs[i], where[i], sems.at[i]) for i in range(n_found)]
        for copy in copies:
            copy.start()
        acc[...] = so_far_refs[0][...] if n_so_far else jnp.zeros_like(acc)
        if total is not None:
            squares = part_refs[0][in_blocks].astype(F32)
            for ref in part_refs[1:]:
                squares = squares + ref[in_blocks].astype(F32)
            scale = lax.rsqrt(jnp.sum(squares, axis=1, keepdims=True) / total + 1e-6)

        def gather_operand(i, carry):
            value = part_refs[0][i].astype(F32)
            for ref in part_refs[1:]:
                value = value + ref[i].astype(F32)
            if total is not None:
                value = value * scale
            operand[i] = value.astype(BF)
            if want_value:
                value_refs[0][i] = value.astype(BF)
            return carry + value * value if want_sum else carry

        squares = lax.fori_loop(
            0, in_blocks, gather_operand, jnp.zeros((width, size), F32) if want_sum else 0, unroll=4)
        if want_sum:
            left = jnp.broadcast_to(jnp.sum(squares, axis=1, keepdims=True), (width, size))
            lane = lax.broadcasted_iota(jnp.int32, (width, size), 1)
            term = jnp.zeros((width, size), F32)
            for k in range(3):
                rounded = left.astype(BF).astype(F32)
                term = jnp.where(lane == k, rounded, term)
                left = left - rounded
            out_refs[0][out_blocks] = term.astype(BF)
        for copy in copies:
            copy.wait()
        blocks = [(ref, i) for ref in tile_refs for i in range(ref.shape[0])][skip:]
        for count, which, dx, dz, dc, first in groups:
            for s in range(count):
                ref, i = blocks.pop(0)
                at_row = where[which][dc, 0, first + s]
                at_col = where[which][dc, 1, first + s] + (2 * dz + dc) * col_blocks
                live = at_row >= 0
                if backward:
                    to = jnp.where(live, at_col, out_blocks)
                    source = jnp.maximum(at_row, 0) + dx * row_blocks
                else:
                    to = jnp.where(live, at_row + dx * row_blocks, out_blocks)
                    source = at_col
                acc[to] += lax.dot_general(operand[source], ref[i], contract, preferred_element_type=F32)
        if not want_acc:
            part = width // split
            for k, ref in enumerate(out_refs):
                ref[0:out_blocks] = acc[0:out_blocks, k * part:(k + 1) * part, :].astype(BF)

    acc_shape = (out_blocks + 1, width, size)
    if want_acc:
        out_shape = [pltpu.VMEM(acc_shape, F32)]
    else:
        out_shape = [pltpu.VMEM((out_blocks + int(want_sum), width // split, size), BF)] * split
    if want_value:
        out_shape.append(pltpu.VMEM((in_blocks, width, size), BF))
    vmem = pl.BlockSpec(memory_space=pltpu.VMEM)
    others = [*tiles, *parts] + ([so_far] if n_so_far else [])
    return pl.pallas_call(
        body,
        out_shape=out_shape,
        in_specs=[pl.BlockSpec(memory_space=pl.ANY)] * n_found + [vmem] * len(others),
        out_specs=[vmem] * len(out_shape),
        scratch_shapes=[
            pltpu.VMEM((in_blocks, width, size), BF),
            pltpu.VMEM((8, 128) if want_acc else acc_shape, F32),
        ]
        + [pltpu.SMEM(f.shape, jnp.int32) for f in found]
        + [pltpu.SemaphoreType.DMA((n_found,))],
        compiler_params=pltpu.CompilerParams(vmem_limit_bytes=8 * 1024 * 1024),
        name="product",
    )(*found, *[in_vmem(t) for t in others])


def pack(values, basis, spans, rows, row_blocks, col_blocks):
    count = len(values)
    terms = len(basis[0])
    _, part, size = values[0].shape
    width = part * count

    def body(*refs):
        value_refs = refs[:count]
        basis_refs = [refs[count + terms * k:count + terms * (k + 1)] for k in range(count)]
        keep_ref, other_ref, squares_ref, summed = refs[count * (terms + 1):]
        row, col = lax.axis_index("row"), lax.axis_index("col")
        x, z, core = row % 2, (col // 2) % 2, col % 2
        for k in range(count):
            def add(i, carry, k=k):
                value = basis_refs[k][0][i].astype(F32)
                for ref in basis_refs[k][1:]:
                    value = value + ref[i].astype(F32)
                summed[i, k * part:(k + 1) * part, :] = value
                return carry + value * value

            squares = lax.fori_loop(0, 4 * col_blocks, add, jnp.zeros((part, size), F32), unroll=4)
            squares_ref[k * part:(k + 1) * part, :] = squares
        for dx in range(2):
            for dz in range(2):
                for dc, ref in ((0, keep_ref), (1, other_ref)):
                    at = 4 * (col // 4) + 2 * jnp.bitwise_xor(z, dz) + jnp.bitwise_xor(core, dc)
                    first = dx * row_blocks + at * rows[0] // size
                    for b in range(spans[0]):
                        for k in range(count):
                            ref[dx, dz, b, k * part:(k + 1) * part, :] = value_refs[k][first + b]
                    at = 2 * (row // 2) + jnp.bitwise_xor(x, dx)
                    first = (2 * dz + dc) * col_blocks + at * rows[1] // size
                    for b in range(spans[1]):
                        ref[dx, dz, spans[0] + b] = summed[first + b].astype(BF)

    vmem = pl.BlockSpec(memory_space=pltpu.VMEM)
    operands = [*values, *[t for b in basis for t in b]]
    return pl.pallas_call(
        body,
        out_shape=[pltpu.VMEM((2, 2, sum(spans), width, size), BF)] * 2 + [pltpu.VMEM((width, size), F32)],
        in_specs=[vmem] * len(operands),
        out_specs=[vmem] * 3,
        scratch_shapes=[pltpu.VMEM((4 * col_blocks, width, size), F32)],
        compiler_params=pltpu.CompilerParams(vmem_limit_bytes=8 * 1024 * 1024),
        name="pack",
    )(*[in_vmem(t) for t in operands])


def assemble(messages, spans):
    _, blocks, width, size = messages[0][0].shape
    flat = [messages[dx][dz] for dx in range(2) for dz in range(2)]

    def body(*refs):
        image_ref, basis_ref, scratch = refs[4:]
        x = lax.axis_index("row") % 2
        z = (lax.axis_index("col") // 2) % 2
        core = lax.axis_index("col") % 2
        for dx in range(2):
            for dz in range(2):
                for dc in range(2):
                    at = 4 * jnp.bitwise_xor(x, dx) + 2 * jnp.bitwise_xor(z, dz) + jnp.bitwise_xor(core, dc)
                    at = pl.multiple_of(at * width, width)
                    for b in range(blocks):
                        scratch[b, pl.ds(at, width), :] = refs[2 * dx + dz][dc, b].astype(F32)
        for b in range(blocks):
            ref, row = (image_ref, b) if b < spans[0] else (basis_ref, b - spans[0])
            ref[row * size:(row + 1) * size, :] = scratch[b].T.astype(BF)

    vmem = pl.BlockSpec(memory_space=pltpu.VMEM)
    return pl.pallas_call(
        body,
        out_shape=[jax.ShapeDtypeStruct((span * size, 8 * width), BF) for span in spans],
        in_specs=[vmem] * 4,
        out_specs=[vmem] * 2,
        scratch_shapes=[pltpu.VMEM((blocks, 8 * width, size), F32)],
        compiler_params=pltpu.CompilerParams(vmem_limit_bytes=8 * 1024 * 1024),
        name="assemble",
    )(*[in_vmem(m) for m in flat])


def shards(n_row, n_col, slab_rows, block_tiles, block_rows, block_cols, counts, start_basis):
    tiles = block_tiles[0]
    slots, size, _ = tiles.shape
    slab_cols, rank = start_basis.shape
    row_blocks = slab_rows // size
    col_blocks = slab_cols // size
    width = rank // 8

    def send(value, dx, dz, dc):
        return lax.ppermute(value, ("row", "col"), [
            (r * n_col + c, (r ^ dx) * n_col + (c ^ (2 * dz + dc)))
            for r in range(n_row) for c in range(n_col)])

    def others_z(value):
        return [
            lax.ppermute(value, "col", [(c, (c + 4 * k) % n_col) for c in range(n_col)])
            for k in range(1, n_col // 4)
        ]

    def others_row(value):
        return [
            lax.ppermute(value, "row", [(r, (r + 2 * k) % n_row) for r in range(n_row)])
            for k in range(1, n_row // 2)
        ]

    cut = slots // 2
    late = slots - slots // 4
    keep, other, tiles_0, tiles_1 = first_product(
        block_rows, block_cols, counts, start_basis, tiles, row_blocks, cut)
    image = keep.astype(F32) + send(other, 0, 0, 1).astype(F32)
    image = image.astype(BF).reshape(2, 2, row_blocks, width, size)
    image = (image[:, 0].astype(F32) + send(image[:, 1], 0, 1, 0).astype(F32)).astype(BF)
    image = jnp.concatenate([image[0], send(image[1], 1, 0, 0)])
    image = [image] + others_z(image)

    tiles_x0 = send(tiles_0, 1, 0, 0)
    tiles_x1 = send(tiles_1, 1, 0, 0)
    tiles_z0 = send(tiles_0, 0, 1, 0)
    tiles_z1 = send(tiles_1, 0, 1, 0)
    corner_0 = send(tiles_z0, 1, 0, 0)
    corner_1 = send(tiles_z1[:late - cut], 1, 0, 0)
    corner_2 = send(tiles_x1[late - cut:], 0, 1, 0)

    block_rows, block_cols, counts, _ = lax.optimization_barrier((block_rows, block_cols, counts, other))
    own = jnp.stack([
        jnp.where(jnp.arange(slots, dtype=jnp.int32) < counts[0, 0], block_rows[0], -1), block_cols[0]])
    own = jnp.stack([own, send(own, 0, 0, 1)])
    found = [own, send(own, 1, 0, 0), send(own, 0, 1, 0), send(own, 1, 1, 0)]

    blocks, groups = [], []
    for some, which, dx, dz, at in (
        (tiles_0, 0, 0, 0, 0), (tiles_1, 0, 0, 0, cut), (tiles_x0, 1, 1, 0, 0),
        (tiles_x1, 1, 1, 0, cut), (tiles_z0, 2, 0, 1, 0), (tiles_z1, 2, 0, 1, cut),
        (corner_0, 3, 1, 1, 0), (corner_1, 3, 1, 1, cut), (corner_2, 3, 1, 1, late)):
        blocks += [some, send(some, 0, 0, 1)]
        groups += [(some.shape[0], which, dx, dz, dc, at) for dc in range(2)]

    total = n_col * slab_cols
    product = functools.partial(block_product, row_blocks=row_blocks, col_blocks=col_blocks)
    (near,) = product(True, found[:3], blocks[:12], groups[:12], image, want_acc=True)
    corner = [(g[0], 0, *g[2:]) for g in groups[12:]]
    basis = product(True, found[3:], blocks[12:], corner, image, so_far=near, split=2)
    both = flip_blocks(blocks)
    as_they_are = both.shape[0] // 2

    basis = [[b] + others_row(b) for b in basis]
    image = []
    for b in basis:
        (out,) = product(False, found, [both], groups, b, want_sum=True)
        image.append([out] + others_z(out))
    basis, values = [], []
    for i in image:
        out, value = product(True, found, [both], groups, i, total=total, want_value=True, skip=as_they_are)
        values.append(value)
        basis.append([out] + others_row(out))
    image_rows = slab_rows // n_col
    basis_rows = slab_cols // n_row
    image_span = max(image_rows // size, 1)
    basis_span = max(basis_rows // size, 1)
    keep, other, squares = pack(
        values, basis, (image_span, basis_span), (image_rows, basis_rows), row_blocks, col_blocks)

    twin_squares = [
        lax.ppermute(squares, "col", [(c, (c + 4 * k) % n_col ^ 1) for c in range(n_col)])
        for k in range(1, n_col // 4)
    ]
    twin_squares = functools.reduce(jnp.add, twin_squares + [send(squares, 0, 0, 1)])
    squares = functools.reduce(jnp.add, [squares] + others_z(squares))

    twin = send(other, 0, 0, 1)

    def scaled(piece, sums):
        factor = lax.rsqrt(jnp.sum(sums, axis=1, keepdims=True) / total + 1e-6)
        factor = jnp.broadcast_to(factor, (basis_span, width, 1))
        factor = jnp.concatenate([jnp.ones((image_span, width, 1), F32), factor])
        return (piece.astype(F32) * factor).astype(BF)

    messages = [[jnp.stack([scaled(keep[dx, dz], squares), scaled(twin[dx, dz], twin_squares)]) for dz in range(2)] for dx in range(2)]
    messages = [
        [messages[0][0], send(messages[0][1], 0, 1, 0)], [send(messages[1][0], 1, 0, 0), send(messages[1][1], 1, 1, 0)]
    ]
    image_piece, basis_piece = assemble(messages, (image_span, basis_span))
    if image_rows < size:
        image_piece = lax.dynamic_slice_in_dim(image_piece, lax.axis_index("col") * image_rows % size, image_rows, 0)
    if basis_rows < size:
        basis_piece = lax.dynamic_slice_in_dim(basis_piece, lax.axis_index("row") * basis_rows % size, basis_rows, 0)
    return image_piece, basis_piece


def solution(mesh):
    n_row, n_col = mesh.shape["row"], mesh.shape["col"]

    def whole(block_tiles, block_rows, block_cols, counts, start_basis):
        slab_rows = start_basis.shape[0] // n_row
        return jax.shard_map(
            functools.partial(shards, n_row, n_col, slab_rows),
            mesh=mesh,
            in_specs=(
                P("row", "col", None, None),
                P("row", "col"),
                P("row", "col"),
                P("row", "col"),
                P("col", None),
            ),
            out_specs=(P(("row", "col"), None), P(("col", "row"), None)),
            check_vma=False,
        )(block_tiles, block_rows, block_cols, counts, start_basis)

    return whole
```
